32 devices in a mesh: group: 2 (over y), tensor: 4 (over z), section: 4 (over x, core).
Axes of the slice: x: 2, y: 2, z: 4, core: 2. Of those that a mesh axis runs over, the one named last changes fastest.
Arguments:
- stream_in: bfloat16 [4, 136, 4096], P('section', 'group', 'tensor'), parts along dimension 1, may hold values from -6 to 6
- pend_in: bfloat16 [4, 136, 4096], P('section', 'group', 'tensor'), parts along dimension 1, may hold values from -6 to 6
- arrivals: bfloat16 [2, 136, 4096], P(None, 'group', 'tensor'), parts along dimension 1, may hold values from -6 to 6
- norm_gain: float32 [4, 4096], P('section'), may hold values from 0.25 to 1.75
- wq: bfloat16 [4, 4096, 512], P('section', None, 'tensor'), may hold values from -11.25 to 11.25
- wkv: bfloat16 [4, 4096, 1024], P('section', None, 'tensor'), may hold values from -0.09375 to 0.09375
- wo: bfloat16 [4, 512, 4096], P('section', 'tensor'), may hold values from -0.5 to 0.5
- cache: bfloat16 [4, 6, 4, 384, 1024], P('section', 'group', 'tensor'), parts along dimension 1, may hold values from -6 to 6
- dec_len: int32 [12, 4], P('group', 'tensor'), parts along dimension 0, may hold values from 1 to 384, as said below
- span_seg: int32 [12, 64], P('group'), parts along dimension 0, may hold values from 0 to 3, never falling along the last dimension, each value on 1 to 32 neighbouring positions
Outputs:
- hist_stream: bfloat16 [4, 3, 136, 4096], P('section', None, 'group', 'tensor'), parts along dimension 2
- hist_pend: bfloat16 [4, 3, 136, 4096], P('section', None, 'group', 'tensor'), parts along dimension 2
The draws below stay inside these ranges and needn't reach their ends.
There are 2 independent parts, one for each index of `group`. The reference program is written for one: setup_inputs(seed, part) draws one part's arguments, and reference() takes and returns one part's arrays. A program takes and returns all parts, laid end to end along the dimension named above; an argument that names none is the same for every part. Nothing has to cross between parts.
Inputs may be any that keep to these rules, and one draw needn't show every extreme that they name: `dec_len`: every micro-batch has some decode row with a full cache of 384 live positions.
All inputs are finite; a program needn't handle non-finite values.
Results may differ from the reference program's by a relative error of at most 0.03.
The reference program's roundings to bfloat16 on the way (of `stream`, `normed`, `span_out`, `dec_out`, `pending_new` and `stream_new`) count: a program that leaves them out, or rounds other values in their place, can miss the bound.
Values may be sent and summed in bfloat16 or wider, within the bound.
No kernel may reach another device: no remote copies, remote signals or barrier semaphores. Data moves between devices by JAX's collectives and lax.ppermute only.
A program may use at most 64 MiB of HBM per device.

```python
import math
import jax
import jax.numpy as jnp
import numpy as np
from jax import lax

D = 4096
HD = 128
KV_HEADS = 4
SPAN = 64
CACHE = 384
TICKS = 3
HEADS = 4
KVC = 1024
DEC = 4
ROWS = 68
MICRO = 6
N_SECTION = 4


def draw_dec_len(key, part):
    first, second = jax.random.split(jax.random.fold_in(key, 17))
    base = jax.random.randint(first, (MICRO, DEC), 1, CACHE + 1)
    chosen = jax.random.randint(second, (MICRO, 1), 0, DEC)
    columns = jnp.arange(DEC, dtype=jnp.int32)[None, :]
    return jnp.where(columns == chosen, CACHE, base).astype(jnp.int32)


def draw_wq(key, part):
    first = jax.random.fold_in(jax.random.fold_in(key, 29), 0)
    base = jax.random.truncated_normal(first, -6.0, 6.0, (N_SECTION, D, HEADS * HD), jnp.float32)
    base = base * float(D) ** (-0.5)
    return base.astype(jnp.bfloat16)


def level_of(rng, extent, pieces, smallest, high):
    loudness = 1.0
    for position, parts in pieces:
        steps = jax.random.uniform(jax.random.fold_in(jax.random.fold_in(rng, 6), position), (parts,), jnp.float32, smallest / len(pieces), high / len(pieces))
        loudness = loudness * jnp.repeat(jnp.exp(steps), extent[position] // parts).reshape((-1,) + (1,) * (len(extent) - 1 - position))
    return loudness


def profile(number_of, total, bound, slope):
    loads = [(1 << 20) // math.isqrt(grade ** slope) + 1 for grade in range(2, number_of + 1)]
    spare, counts = total - bound - (number_of - 1), [1] * (number_of - 1)
    while spare > 0:
        candidates = [i for i in range(number_of - 1) if counts[i] < bound]
        whole, left = sum([loads[i] for i in candidates]), spare
        for i in candidates:
            addition = min(bound - counts[i], max(1, left * loads[i] // whole), spare)
            counts[i] = counts[i] + addition
            spare = spare - addition
    return np.array([bound] + counts)


def uneven(rng, number_of, total, most, skew):
    if number_of == 2:
        one = jax.random.randint(rng, (), max(1, total - most), min(most, total - 1) + 1)
        return jnp.stack([one, total - one])
    tallies = jnp.asarray(profile(number_of, total, most, skew), jnp.int32)
    twos = (number_of - 1) // 2
    source_of, taker = tallies[1:1 + 2 * twos:2], tallies[2:2 + 2 * twos:2]
    slack = jnp.minimum(source_of - 1, most - taker)
    shifted = jax.random.randint(jax.random.fold_in(rng, 1), (twos,), 0, 1 << 20) % (slack + 1)
    tallies = tallies.at[1:1 + 2 * twos:2].set(source_of - shifted).at[2:2 + 2 * twos:2].set(taker + shifted)
    return tallies[jax.random.permutation(jax.random.fold_in(rng, 2), number_of)]


def gaussian(key, shape, deviation, limit, cuts=(), kind=jnp.bfloat16):
    drawn = jax.random.normal(key, shape, jnp.float32) * deviation
    if len(cuts) > 0:
        drawn = level_of(key, shape, cuts, -0.22, 0.18) * drawn
    return jnp.clip(drawn, min=-limit, max=limit).astype(kind)


def setup_inputs(seed: int = 0, part: int = 0) -> dict:
    key_list = jax.random.split(jax.random.key(seed), 11)
    part_keys = jax.random.split(jax.random.fold_in(key_list[10], part), 11)
    return {
        "stream_in": gaussian(part_keys[0], (N_SECTION, ROWS, D), 1.0, 6.0, ((0, 4), (2, 4))),
        "pend_in": gaussian(part_keys[1], (N_SECTION, ROWS, D), 1.0, 6.0, ((0, 4), (2, 4))),
        "arrivals": gaussian(part_keys[2], (TICKS - 1, ROWS, D), 1.0, 6.0, ((2, 4),)),
        "norm_gain": jnp.clip(1.0 + 0.15 * jax.random.normal(key_list[3], (N_SECTION, D), jnp.float32), 0.25, 1.75),
        "wq": draw_wq(jax.random.fold_in(key_list[10], 71), part),
        "wkv": gaussian(key_list[5], (N_SECTION, D, KVC), D ** -0.5, 0.09375, ((0, 4), (2, 4))),
        "wo": gaussian(key_list[6], (N_SECTION, HEADS * HD, D), (HEADS * HD // 4) ** -0.5, 0.5, ((0, 4), (1, 4))),
        "cache": gaussian(part_keys[7], (N_SECTION, TICKS, DEC, CACHE, KVC), 1.0, 6.0, ((0, 4), (2, 4))),
        "dec_len": draw_dec_len(jax.random.fold_in(jax.random.fold_in(key_list[10], part), 71), part),
        "span_seg": jax.vmap(lambda own: jnp.searchsorted(jnp.cumsum(uneven(own, 4, SPAN, SPAN // 2, 1)), jnp.arange(SPAN), side="right"))(jax.random.split(part_keys[9], MICRO)).reshape((MICRO, SPAN)).astype(jnp.int32),
    }


EPS = 1e-05
NEG = -1e+30

def rms_norm(stream, gain):
    values = stream.astype(jnp.float32)
    mean_sq = lax.optimization_barrier(jnp.mean(values * values, axis=-1, keepdims=True))
    return (values * lax.rsqrt(mean_sq + EPS) * gain).astype(jnp.bfloat16)

def span_attention(queries, keys, values, segment):
    scale = 1.0 / math.sqrt(queries.shape[-1])
    scores = jnp.einsum('qgjd,kgd->gjqk', queries.astype(jnp.float32), keys.astype(jnp.float32)) * scale
    count = segment.shape[0]
    rowsid = lax.broadcasted_iota(jnp.int32, (count, count), 0)
    colsid = lax.broadcasted_iota(jnp.int32, (count, count), 1)
    allowed = (segment[:, None] == segment[None, :]) & (colsid <= rowsid)
    scores = jnp.where(allowed, scores, NEG)
    top = lax.optimization_barrier(jnp.max(scores, axis=-1, keepdims=True))
    expo = jnp.exp(scores - top)
    weights = (expo / lax.optimization_barrier(jnp.sum(expo, axis=-1, keepdims=True))).astype(jnp.bfloat16)
    result = jnp.einsum('gjqk,kgd->qgjd', weights.astype(jnp.float32), values.astype(jnp.float32))
    return result.astype(jnp.bfloat16)

def decode_attention(queries, cache_keys, cache_values, new_keys, new_values, lengths):
    scale = 1.0 / math.sqrt(queries.shape[-1])
    qfloat = queries.astype(jnp.float32)
    scores = jnp.einsum('rgjd,rcgd->rgjc', qfloat, cache_keys.astype(jnp.float32)) * scale
    positions = lax.broadcasted_iota(jnp.int32, scores.shape, 3)
    scores = jnp.where(positions < lengths[:, None, None, None], scores, NEG)
    own = jnp.einsum('rgjd,rgd->rgj', qfloat, new_keys.astype(jnp.float32)) * scale
    top = jnp.maximum(lax.optimization_barrier(jnp.max(scores, axis=-1)), own)
    expo = jnp.exp(scores - top[..., None])
    own_expo = jnp.exp(own - top)
    total = lax.optimization_barrier(jnp.sum(expo, axis=-1)) + own_expo
    weights = (expo / total[..., None]).astype(jnp.bfloat16)
    own_weight = (own_expo / total).astype(jnp.bfloat16)
    result = jnp.einsum('rgjc,rcgd->rgjd', weights.astype(jnp.float32), cache_values.astype(jnp.float32))
    result = result + own_weight.astype(jnp.float32)[..., None] * new_values.astype(jnp.float32)[:, :, None, :]
    return result.astype(jnp.bfloat16)

def layer_block(stream, pending, gain, wq_section, wkv_section, wo_section, cache_now, lengths, segment):
    group = HEADS // KV_HEADS
    normed = rms_norm(stream, gain)
    queries = jnp.dot(normed, wq_section, preferred_element_type=jnp.float32).astype(jnp.bfloat16)
    keyval = jnp.dot(normed, wkv_section, preferred_element_type=jnp.float32).astype(jnp.bfloat16)
    queries = queries.reshape(ROWS, KV_HEADS, group, HD)
    keys = keyval[:, :KV_HEADS * HD].reshape(ROWS, KV_HEADS, HD)
    values = keyval[:, KV_HEADS * HD:].reshape(ROWS, KV_HEADS, HD)
    span_out = span_attention(queries[:SPAN], keys[:SPAN], values[:SPAN], segment)
    cache_keys = cache_now[:, :, :KV_HEADS * HD].reshape(DEC, CACHE, KV_HEADS, HD)
    cache_values = cache_now[:, :, KV_HEADS * HD:].reshape(DEC, CACHE, KV_HEADS, HD)
    dec_out = decode_attention(queries[SPAN:], cache_keys, cache_values, keys[SPAN:], values[SPAN:], lengths)
    attended = jnp.concatenate([span_out, dec_out], axis=0).reshape(ROWS, HEADS, HD)
    terms = jnp.einsum('rhd,hde->hre', attended.astype(jnp.float32), wo_section.reshape(HEADS, HD, D).astype(jnp.float32))
    rounded = lax.optimization_barrier(terms.astype(jnp.bfloat16)).astype(jnp.float32)
    pending_new = lax.optimization_barrier(jnp.sum(rounded, axis=0)).astype(jnp.bfloat16)
    stream_new = (stream.astype(jnp.float32) + pending.astype(jnp.float32)).astype(jnp.bfloat16)
    return (stream_new, pending_new)

def reference(stream_in, pend_in, arrivals, norm_gain, wq, wkv, wo, cache, dec_len, span_seg):
    streams = [stream_in[section] for section in range(N_SECTION)]
    pendings = [pend_in[section] for section in range(N_SECTION)]
    hist_stream = [[None] * TICKS for section in range(N_SECTION)]
    hist_pend = [[None] * TICKS for section in range(N_SECTION)]
    for tick in range(TICKS):
        results = []
        for section in range(N_SECTION):
            micro = tick - section + N_SECTION - 1
            out_stream, out_pend = layer_block(streams[section], pendings[section], norm_gain[section], wq[section], wkv[section], wo[section], cache[section, tick], dec_len[micro], span_seg[micro])
            hist_stream[section][tick] = out_stream
            hist_pend[section][tick] = out_pend
            results.append((out_stream, out_pend))
        if tick + 1 < TICKS:
            streams = [arrivals[tick]] + [results[section][0] for section in range(N_SECTION - 1)]
            pendings = [jnp.zeros((ROWS, D), jnp.bfloat16)] + [results[section][1] for section in range(N_SECTION - 1)]
    out_stream = jnp.stack([jnp.stack(hist_stream[section]) for section in range(N_SECTION)])
    out_pend = jnp.stack([jnp.stack(hist_pend[section]) for section in range(N_SECTION)])
    return (out_stream, out_pend)
```

```python
import functools
import math

import jax
import jax.numpy as jnp
from jax import lax
from jax.experimental import pallas as pl
from jax.experimental.pallas import tpu as pltpu
from jax.sharding import PartitionSpec as P

EPS = 1e-05
NEG = -1e30
BF16 = jnp.bfloat16
F32 = jnp.float32


def moved(block, axis, distance):
    devices = range(lax.axis_size(axis))
    route = [(i - distance, i) for i in devices if i - distance in devices]
    return lax.ppermute(block, axis, route)


def turned(block, axis, distance):
    count = lax.axis_size(axis)
    return lax.ppermute(block, axis, [(i, (i + distance) % count) for i in range(count)])


def pieces_of(block, axis):
    return [block] + [turned(block, axis, k) for k in range(1, lax.axis_size(axis))]


def added(left, right):
    return (left.astype(F32) + right.astype(F32)).astype(BF16)


VMEM = pl.BlockSpec(memory_space=pltpu.VMEM)
SMEM = pl.BlockSpec(memory_space=pltpu.SMEM)
ANY = pl.BlockSpec(memory_space=pl.ANY)


def project_kernel(count, span, where_ref, *refs):
    parts = refs[:count]
    gain_ref, wq_ref, wkv_ref, query_ref, message_ref = refs[count:]
    me = where_ref[0]
    shard = parts[0].shape[1]
    rows = parts[0].shape[0]
    total = jnp.zeros((rows, 1), F32)
    for part in parts:
        values = part[...].astype(F32)
        total = total + jnp.sum(values * values, axis=-1, keepdims=True)
    scale = lax.rsqrt(total / (shard * count) + EPS)
    queries = jnp.zeros((rows, wq_ref.shape[1]), F32)
    keyval = jnp.zeros((rows, wkv_ref.shape[1]), F32)
    for k, part in enumerate(parts):
        owner = lax.rem(me - k + count, count)
        start = pl.multiple_of(owner * shard, shard)
        normed = (part[...].astype(F32) * scale * gain_ref[pl.ds(owner, 1), :]).astype(BF16)
        queries = queries + jnp.dot(
            normed, wq_ref[pl.ds(start, shard), :], preferred_element_type=F32
        )
        keyval = keyval + jnp.dot(
            normed, wkv_ref[pl.ds(start, shard), :], preferred_element_type=F32
        )
    queries = queries.astype(BF16)
    query_ref[...] = queries[:span]
    message_ref[:rows] = keyval.astype(BF16)
    base = message_ref.shape[0] - (rows - span)
    message_ref[base:, : queries.shape[1]] = queries[span:]


def attend_kernel(count, span, tick, sections, where_ref, length_ref, *refs):
    parts = refs[1 : 1 + count]
    query_ref = refs[0]
    segment_ref, turned_ref, cache_ref, out_ref, blocks, cached, small, sem = refs[1 + count :]
    me = where_ref[0]
    micro = tick - where_ref[1] + sections - 1
    copy = pltpu.make_async_copy(cache_ref.at[tick], cached, sem)
    copy.start()
    head = query_ref.shape[1]
    factor = 1.0 / math.sqrt(head)
    heads = count
    for k, part in enumerate(parts):
        owner = lax.rem(me - k + count, count)
        blocks[2 * owner] = part[:, :head]
        blocks[2 * owner + 1] = part[:, head:]
    keys = blocks[me, :span]
    values = blocks[heads + me, :span]
    scores = (
        lax.dot_general(
            query_ref[...], keys, (((1,), (1,)), ((), ())), preferred_element_type=F32
        )
        * factor
    )
    across = segment_ref[pl.ds(micro, 1), :]
    lanes = lax.broadcasted_iota(jnp.int32, turned_ref.shape, 1)
    down = jnp.sum(jnp.where(lanes == micro, turned_ref[...], 0), axis=1, keepdims=True)
    row_ids = lax.broadcasted_iota(jnp.int32, (span, span), 0)
    col_ids = lax.broadcasted_iota(jnp.int32, (span, span), 1)
    scores = jnp.where((down == across) & (col_ids <= row_ids), scores, NEG)
    expo = jnp.exp(scores - jnp.max(scores, axis=-1, keepdims=True))
    weights = (expo / jnp.sum(expo, axis=-1, keepdims=True)).astype(BF16)
    out_ref[:span] = jnp.dot(weights, values, preferred_element_type=F32).astype(BF16)
    small[...] = jnp.zeros_like(small)
    last = parts[0].shape[0] - count
    picked = lax.broadcasted_iota(jnp.int32, (count, head), 0) == me

    def own_row(block):
        return jnp.sum(jnp.where(picked, block.astype(F32), 0.0), axis=0, keepdims=True)

    for h in range(heads):
        small[0, h : h + 1, :] = own_row(blocks[2 * h, last:])
        small[1, h : h + 1, :] = own_row(blocks[h, span : span + count])
        small[2, h : h + 1, :] = own_row(blocks[heads + h, span : span + count])
    queries = small[0]
    line = lax.broadcasted_iota(jnp.int32, queries.shape, 0)
    spread = jnp.concatenate(
        [jnp.where(line == h, queries, 0.0) for h in range(heads)], axis=1
    ).astype(BF16)
    own = jnp.sum(queries * small[1], axis=-1, keepdims=True) * factor
    copy.wait()
    dec_scores = (
        lax.dot_general(
            spread,
            cached[:, : heads * head],
            (((1,), (1,)), ((), ())),
            preferred_element_type=F32,
        )
        * factor
    )
    positions = lax.broadcasted_iota(jnp.int32, dec_scores.shape, 1)
    dec_scores = jnp.where(positions < length_ref[micro, 0], dec_scores, NEG)
    top = jnp.maximum(jnp.max(dec_scores, axis=-1, keepdims=True), own)
    dec_expo = jnp.exp(dec_scores - top)
    own_expo = jnp.exp(own - top)
    total = jnp.sum(dec_expo, axis=-1, keepdims=True) + own_expo
    dec_weights = (dec_expo / total).astype(BF16)
    own_weight = (own_expo / total).astype(BF16).astype(F32)
    result = jnp.dot(dec_weights, cached[:, heads * head :], preferred_element_type=F32)
    extra = own_weight * small[2]
    for h in range(heads):
        row = result[h : h + 1, h * head : (h + 1) * head] + extra[h : h + 1]
        small[3, h : h + 1, :] = row
    out_ref[span:] = small[3, :heads].astype(BF16)


def output_kernel(count, span, where_ref, *refs):
    parts = refs[:count]
    weights = refs[count : 2 * count]
    out_ref, rows_ref, decode = refs[2 * count :]
    me = where_ref[0]
    for k, part in enumerate(parts):
        decode[count * k : count * (k + 1)] = part[span:].astype(F32)
    size = count * count
    line = lax.broadcasted_iota(jnp.int32, (size, size), 0)
    lane = lax.broadcasted_iota(jnp.int32, (size, size), 1)
    want_head = lax.rem(me - line // count + count, count)
    from_row = lax.rem(me - lane // count + count, count)
    chosen = (lane % count == want_head) & (line % count == from_row)
    picked = jnp.dot(
        jnp.where(chosen, 1.0, 0.0).astype(BF16),
        decode[...].astype(BF16),
        preferred_element_type=F32,
    )
    total = None
    for k, part in enumerate(parts):
        rows_ref[k, :span] = part[:span]
        rows_ref[k, span : span + count] = picked[count * k : count * (k + 1)].astype(BF16)
        term = jnp.dot(rows_ref[k], weights[k][...], preferred_element_type=F32)
        term = term.astype(BF16).astype(F32)
        total = term if total is None else total + term
    out_ref[...] = total[: span + count].astype(BF16)


def fast_body(
    stream_in, pend_in, arrivals, norm_gain, wq, wkv, wo, cache, dec_len, span_seg
):
    count = lax.axis_size("tensor")
    sections = lax.axis_size("section")
    tensor_index = lax.axis_index("tensor")
    section_index = lax.axis_index("section")
    rows, shard = stream_in.shape[1:]
    head = wq.shape[2]
    span = span_seg.shape[1]
    length = cache.shape[3]
    ticks = cache.shape[1]
    where = jnp.stack([tensor_index, section_index]).astype(jnp.int32)
    gain = norm_gain.reshape(count, shard)
    cached = cache.reshape(ticks, length, cache.shape[4])
    segments = span_seg
    segments_turned = span_seg.T
    message_rows = (rows + 7) // 8 * 8 + count
    limit = pltpu.CompilerParams(vmem_limit_bytes=24 * 1024 * 1024)

    def project(parts):
        return pl.pallas_call(
            functools.partial(project_kernel, count, span),
            out_shape=(
                jax.ShapeDtypeStruct((span, head), BF16),
                jax.ShapeDtypeStruct((message_rows, 2 * head), BF16),
            ),
            in_specs=[SMEM] + [VMEM] * (count + 3),
            out_specs=(VMEM, VMEM),
            compiler_params=limit,
            cost_estimate=pl.CostEstimate(
                flops=2 * rows * shard * count * 3 * head,
                bytes_accessed=2 * shard * count * (3 * head + rows),
                transcendentals=rows,
            ),
            name="project",
        )(where, *parts, gain, wq[0], wkv[0])

    def attend(queries, parts, tick):
        return pl.pallas_call(
            functools.partial(attend_kernel, count, span, tick, sections),
            out_shape=jax.ShapeDtypeStruct((span + count, head), BF16),
            in_specs=[SMEM, SMEM] + [VMEM] * (count + 3) + [ANY],
            out_specs=VMEM,
            scratch_shapes=[
                pltpu.VMEM((2 * count, message_rows, head), BF16),
                pltpu.VMEM((length, cache.shape[4]), BF16),
                pltpu.VMEM((4, 8, head), F32),
                pltpu.SemaphoreType.DMA,
            ],
            compiler_params=limit,
            cost_estimate=pl.CostEstimate(
                flops=4 * 8 * length * 4 * head,
                bytes_accessed=4 * length * 4 * head + count * message_rows * 4 * head,
                transcendentals=span * span,
            ),
            name="attend",
        )(where, dec_len, queries, *parts, segments, segments_turned, cached)

    def output(parts, weights):
        return pl.pallas_call(
            functools.partial(output_kernel, count, span),
            out_shape=jax.ShapeDtypeStruct((rows, shard), BF16),
            in_specs=[SMEM] + [VMEM] * (2 * count),
            out_specs=VMEM,
            scratch_shapes=[
                pltpu.VMEM((count, (rows + 7) // 8 * 8, head), BF16),
                pltpu.VMEM((count * count, head), F32),
            ],
            compiler_params=limit,
            cost_estimate=pl.CostEstimate(
                flops=2 * rows * shard * count * head,
                bytes_accessed=2 * shard * (count * head + rows),
                transcendentals=0,
            ),
            name="output",
        )(where, *parts, *weights)

    stream_parts = pieces_of(stream_in[0], "tensor")
    first_new = added(stream_in[0], pend_in[0])
    one_on = moved(first_new, "section", 1)
    two_on = moved(first_new, "section", 2)
    out_weights = []
    for k in range(count):
        target = lax.rem(tensor_index + k, count)
        block = lax.dynamic_slice_in_dim(wo[0], target * shard, shard, 1)
        out_weights.append(block if k == 0 else turned(block, "tensor", k))
    second = jnp.where(section_index == 0, arrivals[0], one_on)

    queries, message = project(stream_parts)
    attended = attend(queries, pieces_of(message, "tensor"), 0)
    pend_first = output(pieces_of(attended, "tensor"), out_weights)
    pend_two_on = moved(pend_first, "section", 2)
    pend_one_on = moved(pend_first, "section", 1)

    queries, message = project(pieces_of(second, "tensor"))
    attended = attend(queries, pieces_of(message, "tensor"), 1)
    pend_second = output(pieces_of(attended, "tensor"), out_weights)
    second_new = added(second, pend_one_on)
    pend_last_in = moved(pend_second, "section", 1)

    third = jnp.where(
        section_index == 0,
        arrivals[1],
        jnp.where(section_index == 1, arrivals[0], added(two_on, pend_two_on)),
    )
    queries, message = project(pieces_of(third, "tensor"))
    attended = attend(queries, pieces_of(message, "tensor"), 2)
    pend_third = output(pieces_of(attended, "tensor"), out_weights)
    third_new = added(third, pend_last_in)
    return (
        jnp.stack([first_new, second_new, third_new])[None],
        jnp.stack([pend_first, pend_second, pend_third])[None],
    )


def passed_along(block, axis, distance):
    devices = range(lax.axis_size(axis))
    route = [(i - distance, i) for i in devices if i - distance in devices]
    return lax.ppermute(block, axis, route)


def rms_norm(stream, gain):
    values = stream.astype(jnp.float32)
    mean_sq = jnp.mean(values * values, axis=-1, keepdims=True)
    return (values * lax.rsqrt(mean_sq + EPS) * gain).astype(jnp.bfloat16)


def span_attention(queries, keys, values, segment):
    scale = 1.0 / math.sqrt(queries.shape[-1])
    scores = jnp.einsum("qd,kd->qk", queries, keys, preferred_element_type=jnp.float32) * scale
    count = segment.shape[0]
    rowsid = lax.broadcasted_iota(jnp.int32, (count, count), 0)
    colsid = lax.broadcasted_iota(jnp.int32, (count, count), 1)
    allowed = (segment[:, None] == segment[None, :]) & (colsid <= rowsid)
    scores = jnp.where(allowed, scores, NEG)
    top = jnp.max(scores, axis=-1, keepdims=True)
    expo = jnp.exp(scores - top)
    weights = (expo / jnp.sum(expo, axis=-1, keepdims=True)).astype(jnp.bfloat16)
    return jnp.dot(weights, values, preferred_element_type=jnp.float32).astype(jnp.bfloat16)


def decode_attention(queries, cache_keys, cache_values, new_keys, new_values, lengths):
    scale = 1.0 / math.sqrt(queries.shape[-1])
    scores = (
        jnp.einsum("rgjd,rcgd->rgjc", queries, cache_keys, preferred_element_type=jnp.float32)
        * scale
    )
    positions = lax.broadcasted_iota(jnp.int32, scores.shape, 3)
    scores = jnp.where(positions < lengths[:, None, None, None], scores, NEG)
    own = jnp.einsum("rgjd,rgd->rgj", queries, new_keys, preferred_element_type=jnp.float32) * scale
    top = jnp.maximum(jnp.max(scores, axis=-1), own)
    expo = jnp.exp(scores - top[..., None])
    own_expo = jnp.exp(own - top)
    total = jnp.sum(expo, axis=-1) + own_expo
    weights = (expo / total[..., None]).astype(jnp.bfloat16)
    own_weight = (own_expo / total).astype(jnp.bfloat16)
    result = jnp.einsum(
        "rgjc,rcgd->rgjd", weights, cache_values, preferred_element_type=jnp.float32
    )
    result = (
        result
        + own_weight.astype(jnp.float32)[..., None] * new_values.astype(jnp.float32)[:, :, None, :]
    )
    return result.astype(jnp.bfloat16)


def plain_body(stream_in, pend_in, arrivals, norm_gain, wq, wkv, wo, cache, dec_len, span_seg):
    tensor_count = lax.axis_size("tensor")
    section_count = lax.axis_size("section")
    tensor_index = lax.axis_index("tensor")
    section_index = lax.axis_index("section")
    row_count = stream_in.shape[1]
    shard = stream_in.shape[2]
    width = wq.shape[1]
    head_dim = wq.shape[2]
    kv_cols = cache.shape[4]
    kv_heads = kv_cols // (2 * head_dim)
    group_size = tensor_count // kv_heads
    span_rows = span_seg.shape[1]
    dec_rows = cache.shape[2]
    cache_len = cache.shape[3]
    tick_count = cache.shape[1]
    gain = norm_gain[0]
    kv_head = tensor_index // group_size
    stacked = jnp.concatenate([stream_in[0], pend_in[0], arrivals.reshape(-1, shard)], axis=0)
    gathered = lax.all_gather(stacked, "tensor", axis=1, tiled=True)
    stream = gathered[:row_count]
    pending = gathered[row_count : 2 * row_count]
    arrived = gathered[2 * row_count :].reshape(tick_count - 1, row_count, width)
    hist_stream = []
    hist_pend = []
    for tick in range(tick_count):
        micro = tick - section_index + section_count - 1
        lengths = lax.dynamic_index_in_dim(dec_len, micro, 0, keepdims=False)
        segment = lax.dynamic_index_in_dim(span_seg, micro, 0, keepdims=False)
        full_rows = stream
        normed = rms_norm(full_rows, gain)
        queries = jnp.dot(normed, wq[0], preferred_element_type=jnp.float32).astype(jnp.bfloat16)
        kv_part = jnp.dot(normed, wkv[0], preferred_element_type=jnp.float32).astype(jnp.bfloat16)
        keyval = lax.all_gather(kv_part, "tensor", axis=1, tiled=True)
        keys_all = keyval[:span_rows, : kv_heads * head_dim].reshape(span_rows, kv_heads, head_dim)
        values_all = keyval[:span_rows, kv_heads * head_dim :].reshape(
            span_rows, kv_heads, head_dim
        )
        own_keys = lax.dynamic_index_in_dim(keys_all, kv_head, 1, keepdims=False)
        own_values = lax.dynamic_index_in_dim(values_all, kv_head, 1, keepdims=False)
        span_out = span_attention(queries[:span_rows], own_keys, own_values, segment)
        dec_queries = queries[span_rows:].reshape(-1, 1, head_dim)
        row_queries = lax.all_to_all(dec_queries, "tensor", split_axis=0, concat_axis=1, tiled=True)
        row_queries = row_queries.reshape(dec_rows, kv_heads, group_size, head_dim)
        row_start = span_rows + tensor_index * dec_rows
        new_kv = lax.dynamic_slice_in_dim(keyval, row_start, dec_rows, 0)
        new_keys = new_kv[:, : kv_heads * head_dim].reshape(dec_rows, kv_heads, head_dim)
        new_values = new_kv[:, kv_heads * head_dim :].reshape(dec_rows, kv_heads, head_dim)
        cache_now = cache[0, tick]
        cache_keys = cache_now[:, :, : kv_heads * head_dim].reshape(
            dec_rows, cache_len, kv_heads, head_dim
        )
        cache_values = cache_now[:, :, kv_heads * head_dim :].reshape(
            dec_rows, cache_len, kv_heads, head_dim
        )
        row_out = decode_attention(
            row_queries, cache_keys, cache_values, new_keys, new_values, lengths
        )
        row_out = row_out.reshape(dec_rows, tensor_count, head_dim)
        dec_back = lax.all_to_all(
            row_out, "tensor", split_axis=1, concat_axis=0, tiled=True
        ).reshape(-1, head_dim)
        attended = jnp.concatenate([span_out, dec_back], axis=0)
        term = jnp.dot(attended, wo[0], preferred_element_type=jnp.float32).astype(jnp.bfloat16)
        pending_new = lax.psum(term, "tensor").astype(jnp.float32).astype(jnp.bfloat16)
        stream_new = (stream.astype(jnp.float32) + pending.astype(jnp.float32)).astype(jnp.bfloat16)
        hist_stream.append(lax.dynamic_slice_in_dim(stream_new, tensor_index * shard, shard, 1))
        hist_pend.append(lax.dynamic_slice_in_dim(pending_new, tensor_index * shard, shard, 1))
        if tick + 1 < tick_count:
            moved_stream, moved_pend = passed_along((stream_new, pending_new), "section", 1)
            first_section = section_index == 0
            stream = jnp.where(first_section, arrived[tick], moved_stream)
            pending = jnp.where(first_section, jnp.zeros_like(moved_pend), moved_pend)
    return (jnp.stack(hist_stream)[None], jnp.stack(hist_pend)[None])


def body(stream_in, pend_in, arrivals, norm_gain, wq, wkv, wo, cache, dec_len, span_seg):
    count = lax.axis_size("tensor")
    head = wq.shape[2]
    fits = (
        head == 128
        and count <= 8
        and cache.shape[1] == 3
        and cache.shape[2] == 1
        and cache.shape[4] == 2 * head * count
        and wkv.shape[2] == 2 * head
        and stream_in.shape[2] % 128 == 0
        and span_seg.shape[1] % 16 == 0
        and stream_in.shape[1] == span_seg.shape[1] + count
    )
    chosen = fast_body if fits else plain_body
    return chosen(
        stream_in, pend_in, arrivals, norm_gain, wq, wkv, wo, cache, dec_len, span_seg
    )


def solution(mesh):
    return jax.shard_map(
        body,
        mesh=mesh,
        in_specs=(
            P("section", "group", "tensor"),
            P("section", "group", "tensor"),
            P(None, "group", "tensor"),
            P("section", None),
            P("section", None, "tensor"),
            P("section", None, "tensor"),
            P("section", "tensor", None),
            P("section", "group", "tensor", None, None),
            P("group", "tensor"),
            P("group", None),
        ),
        out_specs=(P("section", None, "group", "tensor"), P("section", None, "group", "tensor")),
        check_vma=False,
    )
```

```python
import functools
import math

import jax
import jax.numpy as jnp
from jax import lax
from jax.experimental import pallas as pl
from jax.experimental.pallas import tpu as pltpu
from jax.sharding import PartitionSpec as P

EPS = 1e-05
NEG = -1e30
BF16 = jnp.bfloat16
F32 = jnp.float32


def moved(block, axis, distance):
    devices = range(lax.axis_size(axis))
    route = [(i - distance, i) for i in devices if i - distance in devices]
    return lax.ppermute(block, axis, route)


def turned(block, axis, distance):
    count = lax.axis_size(axis)
    return lax.ppermute(block, axis, [(i, (i + distance) % count) for i in range(count)])


def pieces_of(block, axis):
    return [block] + [turned(block, axis, k) for k in range(1, lax.axis_size(axis))]


def added(left, right):
    return (left.astype(F32) + right.astype(F32)).astype(BF16)


VMEM = pl.BlockSpec(memory_space=pltpu.VMEM)
HBM = pl.BlockSpec(memory_space=pltpu.HBM)
ANY = pl.BlockSpec(memory_space=pl.ANY)


def in_hbm(array):
    return pltpu.with_memory_space_constraint(array, pltpu.HBM)


def in_vmem(array):
    return pltpu.with_memory_space_constraint(array, pltpu.VMEM)


def owner_of(k, count):
    return lax.rem(lax.axis_index("tensor") - k + count, count)


def load_kernel(count, gain_ref, wq_ref, wkv_ref, gain_out, wq_out, wkv_out, sems):
    rows = wq_ref.shape[0] // count
    copies = [pltpu.make_async_copy(gain_ref, gain_out, sems.at[2, 0])]
    for k in range(count):
        part = pl.ds(k * rows, rows)
        copies.append(pltpu.make_async_copy(wq_ref.at[part], wq_out.at[part], sems.at[0, k]))
        copies.append(pltpu.make_async_copy(wkv_ref.at[part], wkv_out.at[part], sems.at[1, k]))
    for copy in copies:
        copy.start()
    for copy in copies:
        copy.wait()


def place_kernel(count, mine_ref, other_ref, weights, sems):
    half = mine_ref.shape[1]
    begin = pl.multiple_of(lax.axis_index("group") * half, half)
    rest = pl.multiple_of(half - lax.axis_index("group") * half, half)
    copies = []
    for h in range(count):
        copies.append(
            pltpu.make_async_copy(
                mine_ref.at[h], weights.at[h, pl.ds(begin, half)], sems.at[0, h]
            )
        )
        copies.append(
            pltpu.make_async_copy(
                other_ref.at[h], weights.at[h, pl.ds(rest, half)], sems.at[1, h]
            )
        )
    for copy in copies:
        copy.start()
    for copy in copies:
        copy.wait()


def project_kernel(count, span, *refs):
    parts = refs[:count]
    gain_ref, wq_ref, wkv_ref, query_ref, message_ref = refs[count:]
    shard = parts[0].shape[1]
    rows = parts[0].shape[0]
    total = jnp.zeros((rows, 1), F32)
    for part in parts:
        values = part[...].astype(F32)
        total = total + jnp.sum(values * values, axis=-1, keepdims=True)
    scale = lax.rsqrt(total / (shard * count) + EPS)
    queries = jnp.zeros((rows, wq_ref.shape[1]), F32)
    keyval = jnp.zeros((rows, wkv_ref.shape[1]), F32)
    for k, part in enumerate(parts):
        here = pl.ds(pl.multiple_of(owner_of(k, count) * shard, shard), shard)
        normed = (part[...].astype(F32) * scale * gain_ref[:, here]).astype(BF16)
        queries = queries + jnp.dot(normed, wq_ref[here, :], preferred_element_type=F32)
        keyval = keyval + jnp.dot(normed, wkv_ref[here, :], preferred_element_type=F32)
    queries = queries.astype(BF16)
    query_ref[...] = queries[:span]
    message_ref[:rows] = keyval.astype(BF16)
    base = message_ref.shape[0] - (rows - span)
    message_ref[base:, : queries.shape[1]] = queries[span:]


def attend_kernel(count, span, tick, *refs):
    query_ref = refs[0]
    parts = refs[1 : 1 + count]
    table_ref, cache_ref, out_ref, blocks, cached, table, small, sem, table_sem = refs[1 + count :]
    me = lax.axis_index("tensor")
    micro = tick - lax.axis_index("section") + lax.axis_size("section") - 1
    table_copy = pltpu.make_async_copy(table_ref.at[pl.ds(micro, 1)], table, table_sem)
    table_copy.start()
    copy = pltpu.make_async_copy(cache_ref.at[tick], cached, sem)
    copy.start()
    head = query_ref.shape[1]
    factor = 1.0 / math.sqrt(head)
    heads = count
    for k, part in enumerate(parts):
        owner = owner_of(k, count)
        blocks[2 * owner] = part[:, :head]
        blocks[2 * owner + 1] = part[:, head : 2 * head]
    keys = blocks[me, :span]
    values = blocks[heads + me, :span]
    scores = (
        lax.dot_general(
            query_ref[...], keys, (((1,), (1,)), ((), ())), preferred_element_type=F32
        )
        * factor
    )
    table_copy.wait()
    across = table[:, :span]
    row_ids = lax.broadcasted_iota(jnp.int32, (span, span), 0)
    col_ids = lax.broadcasted_iota(jnp.int32, (span, span), 1)
    down = jnp.sum(jnp.where(row_ids == col_ids, across, 0), axis=1, keepdims=True)
    scores = jnp.where((down == across) & (col_ids <= row_ids), scores, NEG)
    expo = jnp.exp(scores - jnp.max(scores, axis=-1, keepdims=True))
    weights = (expo / jnp.sum(expo, axis=-1, keepdims=True)).astype(BF16)
    out_ref[:span] = jnp.dot(weights, values, preferred_element_type=F32).astype(BF16)
    small[...] = jnp.zeros_like(small)
    last = parts[0].shape[0] - count
    picked = lax.broadcasted_iota(jnp.int32, (count, head), 0) == me

    def own_row(block):
        return jnp.sum(jnp.where(picked, block.astype(F32), 0.0), axis=0, keepdims=True)

    for h in range(heads):
        small[0, h : h + 1, :] = own_row(blocks[2 * h, last:])
        small[1, h : h + 1, :] = own_row(blocks[h, span : span + count])
        small[2, h : h + 1, :] = own_row(blocks[heads + h, span : span + count])
    queries = small[0]
    line = lax.broadcasted_iota(jnp.int32, queries.shape, 0)
    spread = jnp.concatenate(
        [jnp.where(line == h, queries, 0.0) for h in range(heads)], axis=1
    ).astype(BF16)
    own = jnp.sum(queries * small[1], axis=-1, keepdims=True) * factor
    copy.wait()
    dec_scores = (
        lax.dot_general(
            spread,
            cached[:, : heads * head],
            (((1,), (1,)), ((), ())),
            preferred_element_type=F32,
        )
        * factor
    )
    positions = lax.broadcasted_iota(jnp.int32, dec_scores.shape, 1)
    dec_scores = jnp.where(positions < table[:, span : span + 1], dec_scores, NEG)
    top = jnp.maximum(jnp.max(dec_scores, axis=-1, keepdims=True), own)
    dec_expo = jnp.exp(dec_scores - top)
    own_expo = jnp.exp(own - top)
    total = jnp.sum(dec_expo, axis=-1, keepdims=True) + own_expo
    dec_weights = (dec_expo / total).astype(BF16)
    own_weight = (own_expo / total).astype(BF16).astype(F32)
    result = jnp.dot(dec_weights, cached[:, heads * head :], preferred_element_type=F32)
    extra = own_weight * small[2]
    for h in range(heads):
        row = result[h : h + 1, h * head : (h + 1) * head] + extra[h : h + 1]
        small[3, h : h + 1, :] = row
    out_ref[span:] = small[3, :heads].astype(BF16)


def summed_terms(count, span, parts, weights, scratch):
    rows_ref, decode, placed = scratch
    for k, part in enumerate(parts):
        owner = owner_of(k, count)
        rows_ref[owner, :span] = part[:span]
        decode[owner, :count] = part[span:].astype(F32)
    for h in range(count):
        for r in range(count):
            placed[h, r : r + 1, :] = decode[r, h : h + 1, :]
        rows_ref[h, span : span + count] = placed[h, :count].astype(BF16)
    total = None
    for h in range(count):
        term = jnp.dot(rows_ref[h], weights[h], preferred_element_type=F32)
        term = term.astype(BF16).astype(F32)
        total = term if total is None else total + term
    return total[: span + count].astype(BF16)


def first_output_kernel(count, span, *refs):
    parts = refs[:count]
    weights, out_ref = refs[count : count + 2]
    out_ref[...] = summed_terms(count, span, parts, weights, refs[count + 2 :])


def second_output_kernel(count, span, *refs):
    parts = refs[:count]
    weights, first_new, pend_first, second, pend_in = refs[count : count + 5]
    out_ref, hist_stream, hist_pend = refs[count + 5 : count + 8]
    scratch = refs[count + 8 : -2]
    fresh, sems = refs[-2:]
    fresh[...] = (second[...].astype(F32) + pend_in[...].astype(F32)).astype(BF16)
    copies = [
        pltpu.make_async_copy(first_new, hist_stream.at[0], sems.at[0]),
        pltpu.make_async_copy(fresh, hist_stream.at[1], sems.at[1]),
        pltpu.make_async_copy(pend_first, hist_pend.at[0], sems.at[2]),
    ]
    for copy in copies:
        copy.start()
    out_ref[...] = summed_terms(count, span, parts, weights, scratch)
    last = pltpu.make_async_copy(out_ref, hist_pend.at[1], sems.at[3])
    last.start()
    for copy in copies:
        copy.wait()
    last.wait()


def third_output_kernel(count, span, *refs):
    parts = refs[:count]
    weights, third, pend_in = refs[count : count + 3]
    hist_stream, hist_pend = refs[count + 5 : count + 7]
    scratch = refs[count + 7 : -3]
    fresh, result, sems = refs[-3:]
    fresh[...] = (third[...].astype(F32) + pend_in[...].astype(F32)).astype(BF16)
    copy = pltpu.make_async_copy(fresh, hist_stream.at[2], sems.at[0])
    copy.start()
    result[...] = summed_terms(count, span, parts, weights, scratch)
    last = pltpu.make_async_copy(result, hist_pend.at[2], sems.at[1])
    last.start()
    copy.wait()
    last.wait()


def fast_body(
    stream_in, pend_in, arrivals, norm_gain, wq, wkv, wo, cache, dec_len, span_seg
):
    count = lax.axis_size("tensor")
    section_index = lax.axis_index("section")
    group_index = lax.axis_index("group")
    rows, shard = stream_in.shape[1:]
    head = wq.shape[2]
    span = span_seg.shape[1]
    length = cache.shape[3]
    ticks = cache.shape[1]
    half = head // 2
    cached = in_hbm(cache.reshape(ticks, length, cache.shape[4]))
    table = in_hbm(
        jnp.pad(
            jnp.concatenate([span_seg, dec_len], axis=1),
            ((0, 0), (0, 2 * head - span - 1)),
        )
    )
    padded = (rows + 7) // 8 * 8
    message_rows = padded + count
    limit = pltpu.CompilerParams(vmem_limit_bytes=16 * 1024 * 1024)
    block = jax.ShapeDtypeStruct((rows, shard), BF16)
    history = jax.ShapeDtypeStruct((ticks, rows, shard), BF16)

    def cost(flops, moved_bytes):
        return pl.CostEstimate(
            flops=int(0 * flops), bytes_accessed=int(0 * moved_bytes), transcendentals=0
        )

    gain, wq_here, wkv_here = pl.pallas_call(
        functools.partial(load_kernel, count),
        out_shape=(
            jax.ShapeDtypeStruct(norm_gain.shape, F32),
            jax.ShapeDtypeStruct(wq.shape[1:], BF16),
            jax.ShapeDtypeStruct(wkv.shape[1:], BF16),
        ),
        in_specs=[HBM] * 3,
        out_specs=(VMEM,) * 3,
        scratch_shapes=[pltpu.SemaphoreType.DMA((3, count))],
        compiler_params=limit,
        cost_estimate=cost(0, 4 * wq.shape[1] * 3 * head),
        name="load",
    )(in_hbm(norm_gain), in_hbm(wq[0]), in_hbm(wkv[0]))
    gain, wq_here, wkv_here = in_vmem(gain), in_vmem(wq_here), in_vmem(wkv_here)

    def project(parts):
        return pl.pallas_call(
            functools.partial(project_kernel, count, span),
            out_shape=(
                jax.ShapeDtypeStruct((span, head), BF16),
                jax.ShapeDtypeStruct((message_rows, 2 * head), BF16),
            ),
            in_specs=[VMEM] * (count + 3),
            out_specs=(VMEM, VMEM),
            compiler_params=limit,
            cost_estimate=cost(
                2 * rows * shard * count * 3 * head, 2 * shard * count * (3 * head + rows)
            ),
            name="project",
        )(*[in_vmem(part) for part in parts], gain, wq_here, wkv_here)

    def attend(queries, parts, tick):
        return pl.pallas_call(
            functools.partial(attend_kernel, count, span, tick),
            out_shape=jax.ShapeDtypeStruct((span + count, head), BF16),
            in_specs=[VMEM] * (count + 1) + [HBM] * 2,
            out_specs=VMEM,
            scratch_shapes=[
                pltpu.VMEM((2 * count, message_rows, head), BF16),
                pltpu.VMEM((length, cache.shape[4]), BF16),
                pltpu.VMEM((1, 2 * head), jnp.int32),
                pltpu.VMEM((4, 8, head), F32),
                pltpu.SemaphoreType.DMA,
                pltpu.SemaphoreType.DMA,
            ],
            compiler_params=limit,
            cost_estimate=cost(
                4 * 8 * length * 4 * head,
                4 * length * 4 * head + count * message_rows * 4 * head,
            ),
            name="attend",
        )(queries, *[in_vmem(part) for part in parts], table, cached)

    output_scratch = [
        pltpu.VMEM((count, padded, head), BF16),
        pltpu.VMEM((count, 8, head), F32),
        pltpu.VMEM((count, 8, head), F32),
    ]
    output_cost = cost(2 * rows * shard * count * head, 2 * shard * (count * head + rows))
    barrier = lax.optimization_barrier

    stream_parts = pieces_of(stream_in[0], "tensor")
    own_wo = wo[0]
    own_half = lax.dynamic_slice_in_dim(own_wo, group_index * half, half, 0)
    own_half = own_half.reshape(half, count, shard).transpose(1, 0, 2)
    first_new = added(stream_in[0], pend_in[0])
    one_on = moved(first_new, "section", 1)
    own_half, stream_parts[1] = barrier((own_half, stream_parts[1]))
    mine = lax.all_to_all(own_half, "tensor", split_axis=0, concat_axis=0, tiled=True)
    other = turned(mine, "group", 1)
    weights = in_vmem(
        pl.pallas_call(
            functools.partial(place_kernel, count),
            out_shape=jax.ShapeDtypeStruct((count, head, shard), BF16),
            in_specs=[ANY] * 2,
            out_specs=VMEM,
            scratch_shapes=[pltpu.SemaphoreType.DMA((2, count))],
            compiler_params=limit,
            cost_estimate=cost(0, 4 * count * head * shard),
            name="place",
        )(mine, other)
    )
    early, late = arrivals[0], arrivals[1]
    second = jnp.where(section_index == 0, early, one_on)

    queries, message = project(stream_parts)
    message_parts = pieces_of(message, "tensor")
    attended = attend(queries, message_parts, 0)
    attended_parts = pieces_of(attended, "tensor")
    second, attended = barrier((second, attended))
    second_parts = pieces_of(second, "tensor")
    two_on = moved(first_new, "section", 2)
    base = barrier(
        jnp.where(section_index == 0, late, jnp.where(section_index == 1, early, two_on))
    )
    pend_first = pl.pallas_call(
        functools.partial(first_output_kernel, count, span),
        out_shape=block,
        in_specs=[VMEM] * (count + 1),
        out_specs=VMEM,
        scratch_shapes=output_scratch,
        compiler_params=limit,
        cost_estimate=output_cost,
        name="output_first",
    )(*[in_vmem(part) for part in attended_parts], weights)
    pend_two_on = moved(pend_first, "section", 2)

    queries, message = project(second_parts)
    message_parts = pieces_of(message, "tensor")
    base, message_parts[1] = barrier((base, message_parts[1]))
    third = added(base, pend_two_on)
    third_parts = pieces_of(third, "tensor")
    pend_late = pend_first
    pend_late, third_parts[1] = barrier((pend_late, third_parts[1]))
    pend_one_on = moved(pend_late, "section", 1)
    attended = attend(queries, message_parts, 1)
    attended_parts = pieces_of(attended, "tensor")
    third, attended = barrier((third, attended))
    third_queries, third_message = project([third] + third_parts[1:])
    third_message_parts = pieces_of(third_message, "tensor")
    attended_parts[1], third_message_parts[1] = barrier((attended_parts[1], third_message_parts[1]))
    pend_second, hist_stream, hist_pend = pl.pallas_call(
        functools.partial(second_output_kernel, count, span),
        out_shape=(block, history, history),
        in_specs=[VMEM] * (count + 5),
        out_specs=(VMEM, HBM, HBM),
        scratch_shapes=output_scratch
        + [pltpu.VMEM((rows, shard), BF16), pltpu.SemaphoreType.DMA((4,))],
        compiler_params=limit,
        cost_estimate=output_cost,
        name="output_second",
    )(
        *[in_vmem(part) for part in attended_parts],
        weights,
        in_vmem(first_new),
        in_vmem(pend_first),
        in_vmem(second),
        in_vmem(pend_one_on),
    )
    pend_last_in = moved(pend_second, "section", 1)
    third_queries, pend_second = barrier((third_queries, pend_second))
    attended = attend(third_queries, third_message_parts, 2)
    attended_parts = pieces_of(attended, "tensor")
    hist_stream, hist_pend = pl.pallas_call(
        functools.partial(third_output_kernel, count, span),
        out_shape=(history, history),
        in_specs=[VMEM] * (count + 3) + [HBM] * 2,
        out_specs=(HBM, HBM),
        scratch_shapes=output_scratch
        + [
            pltpu.VMEM((rows, shard), BF16),
            pltpu.VMEM((rows, shard), BF16),
            pltpu.SemaphoreType.DMA((2,)),
        ],
        input_output_aliases={count + 3: 0, count + 4: 1},
        compiler_params=limit,
        cost_estimate=output_cost,
        name="output_third",
    )(
        *[in_vmem(part) for part in attended_parts],
        weights,
        in_vmem(third),
        in_vmem(pend_last_in),
        hist_stream,
        hist_pend,
    )
    return hist_stream[None], hist_pend[None]


def passed_along(block, axis, distance):
    devices = range(lax.axis_size(axis))
    route = [(i - distance, i) for i in devices if i - distance in devices]
    return lax.ppermute(block, axis, route)


def rms_norm(stream, gain):
    values = stream.astype(jnp.float32)
    mean_sq = jnp.mean(values * values, axis=-1, keepdims=True)
    return (values * lax.rsqrt(mean_sq + EPS) * gain).astype(jnp.bfloat16)


def span_attention(queries, keys, values, segment):
    scale = 1.0 / math.sqrt(queries.shape[-1])
    scores = jnp.einsum("qd,kd->qk", queries, keys, preferred_element_type=jnp.float32) * scale
    count = segment.shape[0]
    rowsid = lax.broadcasted_iota(jnp.int32, (count, count), 0)
    colsid = lax.broadcasted_iota(jnp.int32, (count, count), 1)
    allowed = (segment[:, None] == segment[None, :]) & (colsid <= rowsid)
    scores = jnp.where(allowed, scores, NEG)
    top = jnp.max(scores, axis=-1, keepdims=True)
    expo = jnp.exp(scores - top)
    weights = (expo / jnp.sum(expo, axis=-1, keepdims=True)).astype(jnp.bfloat16)
    return jnp.dot(weights, values, preferred_element_type=jnp.float32).astype(jnp.bfloat16)


def decode_attention(queries, cache_keys, cache_values, new_keys, new_values, lengths):
    scale = 1.0 / math.sqrt(queries.shape[-1])
    scores = (
        jnp.einsum("rgjd,rcgd->rgjc", queries, cache_keys, preferred_element_type=jnp.float32)
        * scale
    )
    positions = lax.broadcasted_iota(jnp.int32, scores.shape, 3)
    scores = jnp.where(positions < lengths[:, None, None, None], scores, NEG)
    own = jnp.einsum("rgjd,rgd->rgj", queries, new_keys, preferred_element_type=jnp.float32) * scale
    top = jnp.maximum(jnp.max(scores, axis=-1), own)
    expo = jnp.exp(scores - top[..., None])
    own_expo = jnp.exp(own - top)
    total = jnp.sum(expo, axis=-1) + own_expo
    weights = (expo / total[..., None]).astype(jnp.bfloat16)
    own_weight = (own_expo / total).astype(jnp.bfloat16)
    result = jnp.einsum(
        "rgjc,rcgd->rgjd", weights, cache_values, preferred_element_type=jnp.float32
    )
    result = (
        result
        + own_weight.astype(jnp.float32)[..., None] * new_values.astype(jnp.float32)[:, :, None, :]
    )
    return result.astype(jnp.bfloat16)


def plain_body(stream_in, pend_in, arrivals, norm_gain, wq, wkv, wo, cache, dec_len, span_seg):
    tensor_count = lax.axis_size("tensor")
    section_count = lax.axis_size("section")
    tensor_index = lax.axis_index("tensor")
    section_index = lax.axis_index("section")
    row_count = stream_in.shape[1]
    shard = stream_in.shape[2]
    width = wq.shape[1]
    head_dim = wq.shape[2]
    kv_cols = cache.shape[4]
    kv_heads = kv_cols // (2 * head_dim)
    group_size = tensor_count // kv_heads
    span_rows = span_seg.shape[1]
    dec_rows = cache.shape[2]
    cache_len = cache.shape[3]
    tick_count = cache.shape[1]
    gain = norm_gain[0]
    kv_head = tensor_index // group_size
    stacked = jnp.concatenate([stream_in[0], pend_in[0], arrivals.reshape(-1, shard)], axis=0)
    gathered = lax.all_gather(stacked, "tensor", axis=1, tiled=True)
    stream = gathered[:row_count]
    pending = gathered[row_count : 2 * row_count]
    arrived = gathered[2 * row_count :].reshape(tick_count - 1, row_count, width)
    hist_stream = []
    hist_pend = []
    for tick in range(tick_count):
        micro = tick - section_index + section_count - 1
        lengths = lax.dynamic_index_in_dim(dec_len, micro, 0, keepdims=False)
        segment = lax.dynamic_index_in_dim(span_seg, micro, 0, keepdims=False)
        full_rows = stream
        normed = rms_norm(full_rows, gain)
        queries = jnp.dot(normed, wq[0], preferred_element_type=jnp.float32).astype(jnp.bfloat16)
        kv_part = jnp.dot(normed, wkv[0], preferred_element_type=jnp.float32).astype(jnp.bfloat16)
        keyval = lax.all_gather(kv_part, "tensor", axis=1, tiled=True)
        keys_all = keyval[:span_rows, : kv_heads * head_dim].reshape(span_rows, kv_heads, head_dim)
        values_all = keyval[:span_rows, kv_heads * head_dim :].reshape(
            span_rows, kv_heads, head_dim
        )
        own_keys = lax.dynamic_index_in_dim(keys_all, kv_head, 1, keepdims=False)
        own_values = lax.dynamic_index_in_dim(values_all, kv_head, 1, keepdims=False)
        span_out = span_attention(queries[:span_rows], own_keys, own_values, segment)
        dec_queries = queries[span_rows:].reshape(-1, 1, head_dim)
        row_queries = lax.all_to_all(dec_queries, "tensor", split_axis=0, concat_axis=1, tiled=True)
        row_queries = row_queries.reshape(dec_rows, kv_heads, group_size, head_dim)
        row_start = span_rows + tensor_index * dec_rows
        new_kv = lax.dynamic_slice_in_dim(keyval, row_start, dec_rows, 0)
        new_keys = new_kv[:, : kv_heads * head_dim].reshape(dec_rows, kv_heads, head_dim)
        new_values = new_kv[:, kv_heads * head_dim :].reshape(dec_rows, kv_heads, head_dim)
        cache_now = cache[0, tick]
        cache_keys = cache_now[:, :, : kv_heads * head_dim].reshape(
            dec_rows, cache_len, kv_heads, head_dim
        )
        cache_values = cache_now[:, :, kv_heads * head_dim :].reshape(
            dec_rows, cache_len, kv_heads, head_dim
        )
        row_out = decode_attention(
            row_queries, cache_keys, cache_values, new_keys, new_values, lengths
        )
        row_out = row_out.reshape(dec_rows, tensor_count, head_dim)
        dec_back = lax.all_to_all(
            row_out, "tensor", split_axis=1, concat_axis=0, tiled=True
        ).reshape(-1, head_dim)
        attended = jnp.concatenate([span_out, dec_back], axis=0)
        term = jnp.dot(attended, wo[0], preferred_element_type=jnp.float32).astype(jnp.bfloat16)
        pending_new = lax.psum(term, "tensor").astype(jnp.float32).astype(jnp.bfloat16)
        stream_new = (stream.astype(jnp.float32) + pending.astype(jnp.float32)).astype(jnp.bfloat16)
        hist_stream.append(lax.dynamic_slice_in_dim(stream_new, tensor_index * shard, shard, 1))
        hist_pend.append(lax.dynamic_slice_in_dim(pending_new, tensor_index * shard, shard, 1))
        if tick + 1 < tick_count:
            moved_stream, moved_pend = passed_along((stream_new, pending_new), "section", 1)
            first_section = section_index == 0
            stream = jnp.where(first_section, arrived[tick], moved_stream)
            pending = jnp.where(first_section, jnp.zeros_like(moved_pend), moved_pend)
    return (jnp.stack(hist_stream)[None], jnp.stack(hist_pend)[None])


def body(stream_in, pend_in, arrivals, norm_gain, wq, wkv, wo, cache, dec_len, span_seg):
    count = lax.axis_size("tensor")
    head = wq.shape[2]
    fits = (
        head == 128
        and lax.axis_size("group") == 2
        and count <= 8
        and cache.shape[1] == 3
        and cache.shape[2] == 1
        and cache.shape[4] == 2 * head * count
        and wkv.shape[2] == 2 * head
        and stream_in.shape[2] % 128 == 0
        and span_seg.shape[1] % 16 == 0
        and stream_in.shape[1] == span_seg.shape[1] + count
    )
    chosen = fast_body if fits else plain_body
    return chosen(
        stream_in, pend_in, arrivals, norm_gain, wq, wkv, wo, cache, dec_len, span_seg
    )


def solution(mesh):
    return jax.shard_map(
        body,
        mesh=mesh,
        in_specs=(
            P("section", "group", "tensor"),
            P("section", "group", "tensor"),
            P(None, "group", "tensor"),
            P("section", None),
            P("section", None, "tensor"),
            P("section", None, "tensor"),
            P("section", "tensor", None),
            P("section", "group", "tensor", None, None),
            P("group", "tensor"),
            P("group", None),
        ),
        out_specs=(P("section", None, "group", "tensor"), P("section", None, "group", "tensor")),
        check_vma=False,
    )
```

```python
import functools
import math

import jax
import jax.numpy as jnp
from jax import lax
from jax.experimental import pallas as pl
from jax.experimental.pallas import tpu as pltpu
from jax.sharding import PartitionSpec as P

EPS = 1e-05
NEG = -1e30
BF16 = jnp.bfloat16
F32 = jnp.float32


def moved(block, axis, distance):
    devices = range(lax.axis_size(axis))
    route = [(i - distance, i) for i in devices if i - distance in devices]
    return lax.ppermute(block, axis, route)


def turned(block, axis, distance):
    count = lax.axis_size(axis)
    return lax.ppermute(block, axis, [(i, (i + distance) % count) for i in range(count)])


def pieces_of(block, axis):
    return [block] + [turned(block, axis, k) for k in range(1, lax.axis_size(axis))]


VMEM = pl.BlockSpec(memory_space=pltpu.VMEM)
SMEM = pl.BlockSpec(memory_space=pltpu.SMEM)
HBM = pl.BlockSpec(memory_space=pltpu.HBM)
ANY = pl.BlockSpec(memory_space=pl.ANY)


def in_hbm(array):
    return pltpu.with_memory_space_constraint(array, pltpu.HBM)


def in_vmem(array):
    return pltpu.with_memory_space_constraint(array, pltpu.VMEM)


def owner_of(k, count):
    return lax.rem(lax.axis_index("tensor") - k + count, count)


def load_kernel(count, gain_ref, wq_ref, wkv_ref, gain_out, wq_out, wkv_out, sems):
    rows = wq_ref.shape[0] // count
    copies = [pltpu.make_async_copy(gain_ref, gain_out, sems.at[2, 0])]
    for k in range(count):
        part = pl.ds(k * rows, rows)
        copies.append(pltpu.make_async_copy(wq_ref.at[part], wq_out.at[part], sems.at[0, k]))
        copies.append(pltpu.make_async_copy(wkv_ref.at[part], wkv_out.at[part], sems.at[1, k]))
    for copy in copies:
        copy.start()
    for copy in copies:
        copy.wait()


def begin_kernel(stream_ref, pend_ref, out_ref):
    out_ref[...] = (stream_ref[...].astype(F32) + pend_ref[...].astype(F32)).astype(BF16)


def choose_kernel(arrived_ref, moved_ref, out_ref):
    out_ref[...] = jnp.where(
        lax.axis_index("section") == 0, arrived_ref[...], moved_ref[...]
    )


def cut_kernel(count, wo_ref, *refs):
    blocks, sems = refs[:-1], refs[-1]
    half, shard = blocks[0].shape
    rows = pl.ds(pl.multiple_of(lax.axis_index("group") * half, half), half)
    copies = []
    for k in range(1, count):
        target = lax.rem(lax.axis_index("tensor") + k, count)
        columns = pl.ds(pl.multiple_of(target * shard, shard), shard)
        copies.append(
            pltpu.make_async_copy(wo_ref.at[rows, columns], blocks[k - 1], sems.at[k - 1])
        )
    for copy in copies:
        copy.start()
    for copy in copies:
        copy.wait()


def stack_kernel(*refs):
    out_ref = refs[-1]
    for k, block in enumerate(refs[:-1]):
        out_ref[k] = block[...]


def place_kernel(count, *refs):
    wo_ref = refs[0]
    got = refs[1:count]
    other_ref, weights, sems = refs[count:]
    me, half_index = lax.axis_index("tensor"), lax.axis_index("group")
    half, shard = got[0].shape
    begin = pl.multiple_of(half_index * half, half)
    rest = pl.multiple_of(half - half_index * half, half)
    columns = pl.ds(pl.multiple_of(me * shard, shard), shard)
    copies = [pltpu.make_async_copy(wo_ref.at[:, columns], weights.at[me], sems.at[0, 0])]
    for k in range(1, count):
        owner = owner_of(k, count)
        copies.append(
            pltpu.make_async_copy(
                got[k - 1], weights.at[owner, pl.ds(begin, half)], sems.at[0, k]
            )
        )
        copies.append(
            pltpu.make_async_copy(
                other_ref.at[k - 1], weights.at[owner, pl.ds(rest, half)], sems.at[1, k]
            )
        )
    for copy in copies:
        copy.start()
    for copy in copies:
        copy.wait()


def project_kernel(count, span, batch, *refs):
    parts = refs[: batch * count]
    gain_ref, wq_ref, wkv_ref, query_ref, message_ref = refs[batch * count :]
    rows, shard = parts[0].shape
    block = message_ref.shape[0] // batch
    last = block - (rows - span)
    for b in range(batch):
        own = parts[b * count : (b + 1) * count]
        total = jnp.zeros((rows, 1), F32)
        for part in own:
            values = part[...].astype(F32)
            total = total + jnp.sum(values * values, axis=-1, keepdims=True)
        scale = lax.rsqrt(total / (shard * count) + EPS)
        queries = jnp.zeros((rows, wq_ref.shape[1]), F32)
        keyval = jnp.zeros((rows, wkv_ref.shape[1]), F32)
        for k, part in enumerate(own):
            here = pl.ds(pl.multiple_of(owner_of(k, count) * shard, shard), shard)
            normed = (part[...].astype(F32) * scale * gain_ref[:, here]).astype(BF16)
            queries = queries + jnp.dot(normed, wq_ref[here, :], preferred_element_type=F32)
            keyval = keyval + jnp.dot(normed, wkv_ref[here, :], preferred_element_type=F32)
        queries = queries.astype(BF16)
        query_ref[b] = queries[:span]
        message_ref[b * block : b * block + rows] = keyval.astype(BF16)
        message_ref[b * block + last : (b + 1) * block, : queries.shape[1]] = queries[span:]


def attend_kernel(count, span, ticks, *refs):
    query_ref = refs[0]
    parts = refs[1 : 1 + count]
    segment_ref, length_ref, cache_ref, out_ref, blocks, cached, small, sems = refs[1 + count :]
    me = lax.axis_index("tensor")
    head = query_ref.shape[2]
    factor = 1.0 / math.sqrt(head)
    heads = count
    block = parts[0].shape[0] // len(ticks)
    last = block - count
    copies = []
    for b, tick in enumerate(ticks):
        copy = pltpu.make_async_copy(cache_ref.at[tick], cached.at[b], sems.at[b])
        copy.start()
        copies.append(copy)
    for k, part in enumerate(parts):
        owner = owner_of(k, count)
        blocks[2 * owner] = part[:, :head]
        blocks[2 * owner + 1] = part[:, head:]
    small[...] = jnp.zeros_like(small)
    row_ids = lax.broadcasted_iota(jnp.int32, (span, span), 0)
    col_ids = lax.broadcasted_iota(jnp.int32, (span, span), 1)
    picked = lax.broadcasted_iota(jnp.int32, (count, head), 0) == me

    def own_row(rows):
        return jnp.sum(jnp.where(picked, rows.astype(F32), 0.0), axis=0, keepdims=True)

    for b, tick in enumerate(ticks):
        micro = tick - lax.axis_index("section") + lax.axis_size("section") - 1
        first = b * block
        out = b * (span + count)
        keys = blocks[me, first : first + span]
        values = blocks[heads + me, first : first + span]
        scores = (
            lax.dot_general(
                query_ref[b], keys, (((1,), (1,)), ((), ())), preferred_element_type=F32
            )
            * factor
        )
        across = segment_ref[pl.ds(micro, 1), :]
        down = jnp.sum(jnp.where(row_ids == col_ids, across, 0), axis=1, keepdims=True)
        scores = jnp.where((down == across) & (col_ids <= row_ids), scores, NEG)
        expo = jnp.exp(scores - jnp.max(scores, axis=-1, keepdims=True))
        weights = (expo / jnp.sum(expo, axis=-1, keepdims=True)).astype(BF16)
        out_ref[out : out + span] = jnp.dot(
            weights, values, preferred_element_type=F32
        ).astype(BF16)
        new = slice(first + span, first + span + count)
        for h in range(heads):
            small[b, 0, h : h + 1, :] = own_row(blocks[2 * h, first + last : first + block])
            small[b, 1, h : h + 1, :] = own_row(blocks[h, new])
            small[b, 2, h : h + 1, :] = own_row(blocks[heads + h, new])
        queries = small[b, 0]
        line = lax.broadcasted_iota(jnp.int32, queries.shape, 0)
        spread = jnp.concatenate(
            [jnp.where(line == h, queries, 0.0) for h in range(heads)], axis=1
        ).astype(BF16)
        own = jnp.sum(queries * small[b, 1], axis=-1, keepdims=True) * factor
        copies[b].wait()
        dec_scores = (
            lax.dot_general(
                spread,
                cached[b, :, : heads * head],
                (((1,), (1,)), ((), ())),
                preferred_element_type=F32,
            )
            * factor
        )
        positions = lax.broadcasted_iota(jnp.int32, dec_scores.shape, 1)
        dec_scores = jnp.where(positions < length_ref[0, micro], dec_scores, NEG)
        top = jnp.maximum(jnp.max(dec_scores, axis=-1, keepdims=True), own)
        dec_expo = jnp.exp(dec_scores - top)
        own_expo = jnp.exp(own - top)
        total = jnp.sum(dec_expo, axis=-1, keepdims=True) + own_expo
        dec_weights = (dec_expo / total).astype(BF16)
        own_weight = (own_expo / total).astype(BF16).astype(F32)
        result = jnp.dot(dec_weights, cached[b, :, heads * head :], preferred_element_type=F32)
        extra = own_weight * small[b, 2]
        for h in range(heads):
            row = result[h : h + 1, h * head : (h + 1) * head] + extra[h : h + 1]
            small[b, 3, h : h + 1, :] = row
        out_ref[out + span : out + span + count] = small[b, 3, :heads].astype(BF16)


def summed_terms(count, span, first, parts, weights, scratch):
    rows_ref, decode, placed = scratch
    for k, part in enumerate(parts):
        owner = owner_of(k, count)
        rows_ref[owner, :span] = part[first : first + span]
        decode[owner, :count] = part[first + span : first + span + count].astype(F32)
    for h in range(count):
        for r in range(count):
            placed[h, r : r + 1, :] = decode[r, h : h + 1, :]
        rows_ref[h, span : span + count] = placed[h, :count].astype(BF16)
    total = None
    for h in range(count):
        term = jnp.dot(rows_ref[h], weights[h], preferred_element_type=F32)
        term = term.astype(BF16).astype(F32)
        total = term if total is None else total + term
    return total[: span + count].astype(BF16)


def first_output_kernel(count, span, *refs):
    parts = refs[:count]
    weights, first_new, early, late, out_ref, one_ref, two_ref = refs[count : count + 7]
    section = lax.axis_index("section")
    sections = lax.axis_size("section")
    out_ref[...] = summed_terms(count, span, 0, parts, weights, refs[count + 7 :])
    fresh = (first_new[...].astype(F32) + out_ref[...].astype(F32)).astype(BF16)
    is_last = section == sections - 1
    one_ref[...] = jnp.where(is_last, early[...], fresh)
    two_ref[...] = jnp.where(
        section == sections - 2, late[...], jnp.where(is_last, early[...], fresh)
    )


def second_output_kernel(count, span, *refs):
    parts = refs[:count]
    weights, first_new, pend_first, second_new = refs[count : count + 4]
    out_ref, hist_stream, hist_pend = refs[count + 4 : count + 7]
    scratch = refs[count + 7 : -1]
    sems = refs[-1]
    copies = [
        pltpu.make_async_copy(first_new, hist_stream.at[0], sems.at[0]),
        pltpu.make_async_copy(second_new, hist_stream.at[1], sems.at[1]),
        pltpu.make_async_copy(pend_first, hist_pend.at[0], sems.at[2]),
    ]
    for copy in copies:
        copy.start()
    out_ref[...] = summed_terms(count, span, span + count, parts, weights, scratch)
    last = pltpu.make_async_copy(out_ref, hist_pend.at[1], sems.at[3])
    last.start()
    for copy in copies:
        copy.wait()
    last.wait()


def third_output_kernel(count, span, *refs):
    parts = refs[:count]
    weights, third, pend_in = refs[count : count + 3]
    hist_stream, hist_pend = refs[count + 5 : count + 7]
    scratch = refs[count + 7 : -3]
    fresh, result, sems = refs[-3:]
    fresh[...] = (third[...].astype(F32) + pend_in[...].astype(F32)).astype(BF16)
    copy = pltpu.make_async_copy(fresh, hist_stream.at[2], sems.at[0])
    copy.start()
    result[...] = summed_terms(count, span, 0, parts, weights, scratch)
    last = pltpu.make_async_copy(result, hist_pend.at[2], sems.at[1])
    last.start()
    copy.wait()
    last.wait()


def fast_body(
    stream_in, pend_in, arrivals, norm_gain, wq, wkv, wo, cache, dec_len, span_seg
):
    count = lax.axis_size("tensor")
    rows, shard = stream_in.shape[1:]
    head = wq.shape[2]
    span = span_seg.shape[1]
    length = cache.shape[3]
    ticks = cache.shape[1]
    half = head // 2
    cached = in_hbm(cache.reshape(ticks, length, cache.shape[4]))
    padded = (rows + 7) // 8 * 8
    message_rows = padded + count
    limit = pltpu.CompilerParams(vmem_limit_bytes=16 * 1024 * 1024)
    block = jax.ShapeDtypeStruct((rows, shard), BF16)
    history = jax.ShapeDtypeStruct((ticks, rows, shard), BF16)

    def cost(flops, moved_bytes):
        return pl.CostEstimate(
            flops=int(1 * flops), bytes_accessed=int(1 * moved_bytes), transcendentals=0
        )

    gain, wq_here, wkv_here = pl.pallas_call(
        functools.partial(load_kernel, count),
        out_shape=(
            jax.ShapeDtypeStruct(norm_gain.shape, F32),
            jax.ShapeDtypeStruct(wq.shape[1:], BF16),
            jax.ShapeDtypeStruct(wkv.shape[1:], BF16),
        ),
        in_specs=[HBM] * 3,
        out_specs=(VMEM,) * 3,
        scratch_shapes=[pltpu.SemaphoreType.DMA((3, count))],
        compiler_params=limit,
        cost_estimate=cost(0, 4 * wq.shape[1] * 3 * head),
        name="load",
    )(in_hbm(norm_gain), in_hbm(wq[0]), in_hbm(wkv[0]))
    gain, wq_here, wkv_here = in_vmem(gain), in_vmem(wq_here), in_vmem(wkv_here)

    def project(parts):
        batch = len(parts) // count
        return pl.pallas_call(
            functools.partial(project_kernel, count, span, batch),
            out_shape=(
                jax.ShapeDtypeStruct((batch, span, head), BF16),
                jax.ShapeDtypeStruct((batch * message_rows, 2 * head), BF16),
            ),
            in_specs=[VMEM] * (batch * count + 3),
            out_specs=(VMEM, VMEM),
            compiler_params=limit,
            cost_estimate=cost(
                2 * batch * rows * shard * count * 3 * head,
                2 * shard * count * (3 * head + rows),
            ),
            name="project",
        )(*[in_vmem(part) for part in parts], gain, wq_here, wkv_here)

    def attend(queries, parts, which):
        batch = len(which)
        return pl.pallas_call(
            functools.partial(attend_kernel, count, span, which),
            out_shape=jax.ShapeDtypeStruct((batch * (span + count), head), BF16),
            in_specs=[VMEM] * (count + 2) + [SMEM, HBM],
            out_specs=VMEM,
            scratch_shapes=[
                pltpu.VMEM((2 * count, batch * message_rows, head), BF16),
                pltpu.VMEM((batch, length, cache.shape[4]), BF16),
                pltpu.VMEM((batch, 4, 8, head), F32),
                pltpu.SemaphoreType.DMA((batch,)),
            ],
            compiler_params=limit,
            cost_estimate=cost(
                batch * 4 * 8 * length * 4 * head,
                batch * (4 * length * 4 * head + count * message_rows * 4 * head),
            ),
            name="attend",
        )(queries, *[in_vmem(part) for part in parts], span_seg, dec_len.T, cached)

    output_scratch = [
        pltpu.VMEM((count, padded, head), BF16),
        pltpu.VMEM((count, 8, head), F32),
        pltpu.VMEM((count, 8, head), F32),
    ]
    output_cost = cost(2 * rows * shard * count * head, 2 * shard * (count * head + rows))
    stream_parts = pieces_of(stream_in[0], "tensor")
    first_new = pl.pallas_call(
        begin_kernel,
        out_shape=block,
        in_specs=[VMEM] * 2,
        out_specs=VMEM,
        compiler_params=limit,
        cost_estimate=cost(0, 6 * rows * shard),
        name="begin",
    )(stream_in[0], pend_in[0])
    early, late = arrivals[0], arrivals[1]
    second = pl.pallas_call(
        choose_kernel,
        out_shape=block,
        in_specs=[VMEM] * 2,
        out_specs=VMEM,
        compiler_params=limit,
        cost_estimate=cost(0, 6 * rows * shard),
        name="choose",
    )(early, moved(first_new, "section", 1))
    second_parts = pieces_of(second, "tensor")
    queries, message = project(stream_parts + second_parts)
    message_parts = pieces_of(message, "tensor")
    small_block = jax.ShapeDtypeStruct((half, shard), BF16)
    cut = pl.pallas_call(
        functools.partial(cut_kernel, count),
        out_shape=(small_block,) * (count - 1),
        in_specs=[HBM],
        out_specs=(VMEM,) * (count - 1),
        scratch_shapes=[pltpu.SemaphoreType.DMA((count - 1,))],
        compiler_params=limit,
        cost_estimate=cost(0, 4 * half * shard * count),
        name="cut",
    )(in_hbm(wo[0]))
    blocks = [
        turned(cut[0], "tensor", 1),
        turned(cut[1], "tensor", 2),
        turned(cut[2], "tensor", 3),
    ]
    stacked = pl.pallas_call(
        stack_kernel,
        out_shape=jax.ShapeDtypeStruct((count - 1, half, shard), BF16),
        in_specs=[VMEM] * (count - 1),
        out_specs=VMEM,
        compiler_params=limit,
        cost_estimate=cost(0, 4 * half * shard * count),
        name="stack",
    )(*[in_vmem(block_k) for block_k in blocks])
    given = (in_hbm(wo[0]), *blocks, turned(stacked, "group", 1))
    weights = in_vmem(
        pl.pallas_call(
            functools.partial(place_kernel, count),
            out_shape=jax.ShapeDtypeStruct((count, head, shard), BF16),
            in_specs=[ANY] * len(given),
            out_specs=VMEM,
            scratch_shapes=[pltpu.SemaphoreType.DMA((2, count))],
            compiler_params=limit,
            cost_estimate=cost(0, 4 * count * head * shard),
            name="place",
        )(*given)
    )
    attended = attend(queries, message_parts, (0, 1))
    attended_parts = pieces_of(attended, "tensor")
    pend_first, one_on, two_on = pl.pallas_call(
        functools.partial(first_output_kernel, count, span),
        out_shape=(block, block, block),
        in_specs=[VMEM] * (count + 4),
        out_specs=(VMEM, VMEM, VMEM),
        scratch_shapes=output_scratch,
        compiler_params=limit,
        cost_estimate=output_cost,
        name="output_first",
    )(
        *[in_vmem(part) for part in attended_parts],
        weights,
        in_vmem(first_new),
        in_vmem(early),
        in_vmem(late),
    )
    third = turned(two_on, "section", 2)
    third_parts = pieces_of(third, "tensor")
    second_new = turned(one_on, "section", 1)
    pend_second, hist_stream, hist_pend = pl.pallas_call(
        functools.partial(second_output_kernel, count, span),
        out_shape=(block, history, history),
        in_specs=[VMEM] * (count + 4),
        out_specs=(VMEM, HBM, HBM),
        scratch_shapes=output_scratch + [pltpu.SemaphoreType.DMA((4,))],
        compiler_params=limit,
        cost_estimate=output_cost,
        name="output_second",
    )(
        *[in_vmem(part) for part in attended_parts],
        weights,
        in_vmem(first_new),
        in_vmem(pend_first),
        in_vmem(second_new),
    )
    pend_last_in = moved(pend_second, "section", 1)
    queries, message = project(third_parts)
    message_parts = pieces_of(message, "tensor")
    attended = attend(queries, message_parts, (2,))
    attended_parts = pieces_of(attended, "tensor")
    hist_stream, hist_pend = pl.pallas_call(
        functools.partial(third_output_kernel, count, span),
        out_shape=(history, history),
        in_specs=[VMEM] * (count + 3) + [HBM] * 2,
        out_specs=(HBM, HBM),
        scratch_shapes=output_scratch
        + [
            pltpu.VMEM((rows, shard), BF16),
            pltpu.VMEM((rows, shard), BF16),
            pltpu.SemaphoreType.DMA((2,)),
        ],
        input_output_aliases={count + 3: 0, count + 4: 1},
        compiler_params=limit,
        cost_estimate=output_cost,
        name="output_third",
    )(
        *[in_vmem(part) for part in attended_parts],
        weights,
        in_vmem(third),
        in_vmem(pend_last_in),
        hist_stream,
        hist_pend,
    )
    return hist_stream[None], hist_pend[None]


def passed_along(block, axis, distance):
    devices = range(lax.axis_size(axis))
    route = [(i - distance, i) for i in devices if i - distance in devices]
    return lax.ppermute(block, axis, route)


def rms_norm(stream, gain):
    values = stream.astype(jnp.float32)
    mean_sq = jnp.mean(values * values, axis=-1, keepdims=True)
    return (values * lax.rsqrt(mean_sq + EPS) * gain).astype(jnp.bfloat16)


def span_attention(queries, keys, values, segment):
    scale = 1.0 / math.sqrt(queries.shape[-1])
    scores = jnp.einsum("qd,kd->qk", queries, keys, preferred_element_type=jnp.float32) * scale
    count = segment.shape[0]
    rowsid = lax.broadcasted_iota(jnp.int32, (count, count), 0)
    colsid = lax.broadcasted_iota(jnp.int32, (count, count), 1)
    allowed = (segment[:, None] == segment[None, :]) & (colsid <= rowsid)
    scores = jnp.where(allowed, scores, NEG)
    top = jnp.max(scores, axis=-1, keepdims=True)
    expo = jnp.exp(scores - top)
    weights = (expo / jnp.sum(expo, axis=-1, keepdims=True)).astype(jnp.bfloat16)
    return jnp.dot(weights, values, preferred_element_type=jnp.float32).astype(jnp.bfloat16)


def decode_attention(queries, cache_keys, cache_values, new_keys, new_values, lengths):
    scale = 1.0 / math.sqrt(queries.shape[-1])
    scores = (
        jnp.einsum("rgjd,rcgd->rgjc", queries, cache_keys, preferred_element_type=jnp.float32)
        * scale
    )
    positions = lax.broadcasted_iota(jnp.int32, scores.shape, 3)
    scores = jnp.where(positions < lengths[:, None, None, None], scores, NEG)
    own = jnp.einsum("rgjd,rgd->rgj", queries, new_keys, preferred_element_type=jnp.float32) * scale
    top = jnp.maximum(jnp.max(scores, axis=-1), own)
    expo = jnp.exp(scores - top[..., None])
    own_expo = jnp.exp(own - top)
    total = jnp.sum(expo, axis=-1) + own_expo
    weights = (expo / total[..., None]).astype(jnp.bfloat16)
    own_weight = (own_expo / total).astype(jnp.bfloat16)
    result = jnp.einsum(
        "rgjc,rcgd->rgjd", weights, cache_values, preferred_element_type=jnp.float32
    )
    result = (
        result
        + own_weight.astype(jnp.float32)[..., None] * new_values.astype(jnp.float32)[:, :, None, :]
    )
    return result.astype(jnp.bfloat16)


def plain_body(stream_in, pend_in, arrivals, norm_gain, wq, wkv, wo, cache, dec_len, span_seg):
    tensor_count = lax.axis_size("tensor")
    section_count = lax.axis_size("section")
    tensor_index = lax.axis_index("tensor")
    section_index = lax.axis_index("section")
    row_count = stream_in.shape[1]
    shard = stream_in.shape[2]
    width = wq.shape[1]
    head_dim = wq.shape[2]
    kv_cols = cache.shape[4]
    kv_heads = kv_cols // (2 * head_dim)
    group_size = tensor_count // kv_heads
    span_rows = span_seg.shape[1]
    dec_rows = cache.shape[2]
    cache_len = cache.shape[3]
    tick_count = cache.shape[1]
    gain = norm_gain[0]
    kv_head = tensor_index // group_size
    stacked = jnp.concatenate([stream_in[0], pend_in[0], arrivals.reshape(-1, shard)], axis=0)
    gathered = lax.all_gather(stacked, "tensor", axis=1, tiled=True)
    stream = gathered[:row_count]
    pending = gathered[row_count : 2 * row_count]
    arrived = gathered[2 * row_count :].reshape(tick_count - 1, row_count, width)
    hist_stream = []
    hist_pend = []
    for tick in range(tick_count):
        micro = tick - section_index + section_count - 1
        lengths = lax.dynamic_index_in_dim(dec_len, micro, 0, keepdims=False)
        segment = lax.dynamic_index_in_dim(span_seg, micro, 0, keepdims=False)
        full_rows = stream
        normed = rms_norm(full_rows, gain)
        queries = jnp.dot(normed, wq[0], preferred_element_type=jnp.float32).astype(jnp.bfloat16)
        kv_part = jnp.dot(normed, wkv[0], preferred_element_type=jnp.float32).astype(jnp.bfloat16)
        keyval = lax.all_gather(kv_part, "tensor", axis=1, tiled=True)
        keys_all = keyval[:span_rows, : kv_heads * head_dim].reshape(span_rows, kv_heads, head_dim)
        values_all = keyval[:span_rows, kv_heads * head_dim :].reshape(
            span_rows, kv_heads, head_dim
        )
        own_keys = lax.dynamic_index_in_dim(keys_all, kv_head, 1, keepdims=False)
        own_values = lax.dynamic_index_in_dim(values_all, kv_head, 1, keepdims=False)
        span_out = span_attention(queries[:span_rows], own_keys, own_values, segment)
        dec_queries = queries[span_rows:].reshape(-1, 1, head_dim)
        row_queries = lax.all_to_all(dec_queries, "tensor", split_axis=0, concat_axis=1, tiled=True)
        row_queries = row_queries.reshape(dec_rows, kv_heads, group_size, head_dim)
        row_start = span_rows + tensor_index * dec_rows
        new_kv = lax.dynamic_slice_in_dim(keyval, row_start, dec_rows, 0)
        new_keys = new_kv[:, : kv_heads * head_dim].reshape(dec_rows, kv_heads, head_dim)
        new_values = new_kv[:, kv_heads * head_dim :].reshape(dec_rows, kv_heads, head_dim)
        cache_now = cache[0, tick]
        cache_keys = cache_now[:, :, : kv_heads * head_dim].reshape(
            dec_rows, cache_len, kv_heads, head_dim
        )
        cache_values = cache_now[:, :, kv_heads * head_dim :].reshape(
            dec_rows, cache_len, kv_heads, head_dim
        )
        row_out = decode_attention(
            row_queries, cache_keys, cache_values, new_keys, new_values, lengths
        )
        row_out = row_out.reshape(dec_rows, tensor_count, head_dim)
        dec_back = lax.all_to_all(
            row_out, "tensor", split_axis=1, concat_axis=0, tiled=True
        ).reshape(-1, head_dim)
        attended = jnp.concatenate([span_out, dec_back], axis=0)
        term = jnp.dot(attended, wo[0], preferred_element_type=jnp.float32).astype(jnp.bfloat16)
        pending_new = lax.psum(term, "tensor").astype(jnp.float32).astype(jnp.bfloat16)
        stream_new = (stream.astype(jnp.float32) + pending.astype(jnp.float32)).astype(jnp.bfloat16)
        hist_stream.append(lax.dynamic_slice_in_dim(stream_new, tensor_index * shard, shard, 1))
        hist_pend.append(lax.dynamic_slice_in_dim(pending_new, tensor_index * shard, shard, 1))
        if tick + 1 < tick_count:
            moved_stream, moved_pend = passed_along((stream_new, pending_new), "section", 1)
            first_section = section_index == 0
            stream = jnp.where(first_section, arrived[tick], moved_stream)
            pending = jnp.where(first_section, jnp.zeros_like(moved_pend), moved_pend)
    return (jnp.stack(hist_stream)[None], jnp.stack(hist_pend)[None])


def body(stream_in, pend_in, arrivals, norm_gain, wq, wkv, wo, cache, dec_len, span_seg):
    count = lax.axis_size("tensor")
    head = wq.shape[2]
    fits = (
        head == 128
        and lax.axis_size("group") == 2
        and count <= 8
        and cache.shape[1] == 3
        and cache.shape[2] == 1
        and cache.shape[4] == 2 * head * count
        and wkv.shape[2] == 2 * head
        and stream_in.shape[2] % 128 == 0
        and span_seg.shape[1] % 16 == 0
        and stream_in.shape[1] == span_seg.shape[1] + count
    )
    chosen = fast_body if fits else plain_body
    return chosen(
        stream_in, pend_in, arrivals, norm_gain, wq, wkv, wo, cache, dec_len, span_seg
    )


def solution(mesh):
    return jax.shard_map(
        body,
        mesh=mesh,
        in_specs=(
            P("section", "group", "tensor"),
            P("section", "group", "tensor"),
            P(None, "group", "tensor"),
            P("section", None),
            P("section", None, "tensor"),
            P("section", None, "tensor"),
            P("section", "tensor", None),
            P("section", "group", "tensor", None, None),
            P("group", "tensor"),
            P("group", None),
        ),
        out_specs=(P("section", None, "group", "tensor"), P("section", None, "group", "tensor")),
        check_vma=False,
    )
```

```python
import functools
import math

import jax
import jax.numpy as jnp
from jax import lax
from jax.experimental import pallas as pl
from jax.experimental.pallas import tpu as pltpu
from jax.sharding import PartitionSpec as P

EPS = 1e-05
NEG = -1e30
BF16 = jnp.bfloat16
F32 = jnp.float32


def moved(block, axis, distance):
    devices = range(lax.axis_size(axis))
    route = [(i - distance, i) for i in devices if i - distance in devices]
    return lax.ppermute(block, axis, route)


def turned(block, axis, distance):
    count = lax.axis_size(axis)
    return lax.ppermute(block, axis, [(i, (i + distance) % count) for i in range(count)])


def pieces_of(block, axis):
    return [block] + [turned(block, axis, k) for k in range(1, lax.axis_size(axis))]


def relayed_pieces_of(block, axis):
    if lax.axis_size(axis) != 4:
        return pieces_of(block, axis)
    one = turned(block, axis, 1)
    three = turned(block, axis, 3)
    return [block, one, turned(one, axis, 1), three]


VMEM = pl.BlockSpec(memory_space=pltpu.VMEM)
HBM = pl.BlockSpec(memory_space=pltpu.HBM)
ANY = pl.BlockSpec(memory_space=pl.ANY)


def in_hbm(array):
    return pltpu.with_memory_space_constraint(array, pltpu.HBM)


def in_vmem(array):
    return pltpu.with_memory_space_constraint(array, pltpu.VMEM)


def owner_of(k, count):
    return lax.rem(lax.axis_index("tensor") - k + count, count)


def load_kernel(pieces, *refs):
    given, kept, sems = refs[: len(pieces)], refs[len(pieces) : -1], refs[-1]
    copies = []
    for source, target, count in zip(given, kept, pieces):
        rows = source.shape[0] // count
        for k in range(count):
            part = pl.ds(k * rows, rows)
            copies.append(
                pltpu.make_async_copy(source.at[part], target.at[part], sems.at[len(copies)])
            )
    for copy in copies:
        copy.start()
    for copy in copies:
        copy.wait()


def begin_kernel(stream_ref, pend_ref, out_ref):
    out_ref[...] = (stream_ref[...].astype(F32) + pend_ref[...].astype(F32)).astype(BF16)


def choose_kernel(arrived_ref, moved_ref, out_ref):
    out_ref[...] = jnp.where(
        lax.axis_index("section") == 0, arrived_ref[...], moved_ref[...]
    )


def cut_kernel(count, wo_ref, *refs):
    blocks, sems = refs[:-1], refs[-1]
    half, shard = blocks[0].shape
    rows = pl.ds(pl.multiple_of(lax.axis_index("group") * half, half), half)
    copies = []
    for k in range(1, count):
        target = lax.rem(lax.axis_index("tensor") + k, count)
        columns = pl.ds(pl.multiple_of(target * shard, shard), shard)
        copies.append(
            pltpu.make_async_copy(wo_ref.at[rows, columns], blocks[k - 1], sems.at[k - 1])
        )
    for copy in copies:
        copy.start()
    for copy in copies:
        copy.wait()


def stack_kernel(*refs):
    out_ref = refs[-1]
    for k, block in enumerate(refs[:-1]):
        out_ref[k] = block[...]


def place_kernel(count, *refs):
    wo_ref = refs[0]
    got = refs[1:count]
    other_ref, weights, sems = refs[count:]
    me, half_index = lax.axis_index("tensor"), lax.axis_index("group")
    half, shard = got[0].shape
    begin = pl.multiple_of(half_index * half, half)
    rest = pl.multiple_of(half - half_index * half, half)
    columns = pl.ds(pl.multiple_of(me * shard, shard), shard)
    copies = [pltpu.make_async_copy(wo_ref.at[:, columns], weights.at[me], sems.at[0, 0])]
    for k in range(1, count):
        owner = owner_of(k, count)
        copies.append(
            pltpu.make_async_copy(
                got[k - 1], weights.at[owner, pl.ds(begin, half)], sems.at[0, k]
            )
        )
        copies.append(
            pltpu.make_async_copy(
                other_ref.at[k - 1], weights.at[owner, pl.ds(rest, half)], sems.at[1, k]
            )
        )
    for copy in copies:
        copy.start()
    for copy in copies:
        copy.wait()


def project_kernel(count, span, batch, *refs):
    parts = refs[: batch * count]
    gain_ref, wq_ref, wkv_ref, query_ref, message_ref = refs[batch * count :]
    rows, shard = parts[0].shape
    block = message_ref.shape[0] // batch
    last = block - (rows - span)
    for b in range(batch):
        own = parts[b * count : (b + 1) * count]
        total = jnp.zeros((rows, 1), F32)
        for part in own:
            values = part[...].astype(F32)
            total = total + jnp.sum(values * values, axis=-1, keepdims=True)
        scale = lax.rsqrt(total / (shard * count) + EPS)
        queries = jnp.zeros((rows, wq_ref.shape[1]), F32)
        keyval = jnp.zeros((rows, wkv_ref.shape[1]), F32)
        for k, part in enumerate(own):
            here = pl.ds(pl.multiple_of(owner_of(k, count) * shard, shard), shard)
            normed = (part[...].astype(F32) * scale * gain_ref[:, here]).astype(BF16)
            queries = queries + jnp.dot(normed, wq_ref[here, :], preferred_element_type=F32)
            keyval = keyval + jnp.dot(normed, wkv_ref[here, :], preferred_element_type=F32)
        queries = queries.astype(BF16)
        query_ref[b] = queries[:span]
        message_ref[b * block : b * block + rows] = keyval.astype(BF16)
        message_ref[b * block + last : (b + 1) * block, : queries.shape[1]] = queries[span:]


def attend_kernel(count, span, ticks, *refs):
    query_ref = refs[0]
    parts = refs[1 : 1 + count]
    segment_ref, length_ref, cache_ref, out_ref, blocks, small = refs[1 + count :]
    me = lax.axis_index("tensor")
    head = query_ref.shape[2]
    factor = 1.0 / math.sqrt(head)
    heads = count
    block = parts[0].shape[0] // len(ticks)
    last = block - count
    for k, part in enumerate(parts):
        owner = owner_of(k, count)
        blocks[2 * owner] = part[:, :head]
        blocks[2 * owner + 1] = part[:, head:]
    small[...] = jnp.zeros_like(small)
    row_ids = lax.broadcasted_iota(jnp.int32, (span, span), 0)
    col_ids = lax.broadcasted_iota(jnp.int32, (span, span), 1)
    picked = lax.broadcasted_iota(jnp.int32, (count, head), 0) == me

    def own_row(rows):
        return jnp.sum(jnp.where(picked, rows.astype(F32), 0.0), axis=0, keepdims=True)

    for b, tick in enumerate(ticks):
        micro = tick - lax.axis_index("section") + lax.axis_size("section") - 1
        first = b * block
        out = b * (span + count)
        keys = blocks[me, first : first + span]
        values = blocks[heads + me, first : first + span]
        scores = (
            lax.dot_general(
                query_ref[b], keys, (((1,), (1,)), ((), ())), preferred_element_type=F32
            )
            * factor
        )
        across = segment_ref[pl.ds(micro, 1), :]
        down = jnp.sum(jnp.where(row_ids == col_ids, across, 0), axis=1, keepdims=True)
        scores = jnp.where((down == across) & (col_ids <= row_ids), scores, NEG)
        expo = jnp.exp(scores - jnp.max(scores, axis=-1, keepdims=True))
        weights = (expo / jnp.sum(expo, axis=-1, keepdims=True)).astype(BF16)
        out_ref[out : out + span] = jnp.dot(
            weights, values, preferred_element_type=F32
        ).astype(BF16)
        new = slice(first + span, first + span + count)
        for h in range(heads):
            small[b, 0, h : h + 1, :] = own_row(blocks[2 * h, first + last : first + block])
            small[b, 1, h : h + 1, :] = own_row(blocks[h, new])
            small[b, 2, h : h + 1, :] = own_row(blocks[heads + h, new])
        queries = small[b, 0]
        line = lax.broadcasted_iota(jnp.int32, queries.shape, 0)
        spread = jnp.concatenate(
            [jnp.where(line == h, queries, 0.0) for h in range(heads)], axis=1
        ).astype(BF16)
        own = jnp.sum(queries * small[b, 1], axis=-1, keepdims=True) * factor
        dec_scores = (
            lax.dot_general(
                spread,
                cache_ref[tick, :, : heads * head],
                (((1,), (1,)), ((), ())),
                preferred_element_type=F32,
            )
            * factor
        )
        positions = lax.broadcasted_iota(jnp.int32, dec_scores.shape, 1)
        lanes = lax.broadcasted_iota(jnp.int32, length_ref.shape, 1)
        live = jnp.sum(jnp.where(lanes == micro, length_ref[...], 0), axis=1, keepdims=True)
        dec_scores = jnp.where(positions < live, dec_scores, NEG)
        top = jnp.maximum(jnp.max(dec_scores, axis=-1, keepdims=True), own)
        dec_expo = jnp.exp(dec_scores - top)
        own_expo = jnp.exp(own - top)
        total = jnp.sum(dec_expo, axis=-1, keepdims=True) + own_expo
        dec_weights = (dec_expo / total).astype(BF16)
        own_weight = (own_expo / total).astype(BF16).astype(F32)
        result = jnp.dot(dec_weights, cache_ref[tick, :, heads * head :], preferred_element_type=F32)
        extra = own_weight * small[b, 2]
        for h in range(heads):
            row = result[h : h + 1, h * head : (h + 1) * head] + extra[h : h + 1]
            small[b, 3, h : h + 1, :] = row
        out_ref[out + span : out + span + count] = small[b, 3, :heads].astype(BF16)


def summed_terms(count, span, first, parts, weights, scratch):
    rows_ref, decode, placed = scratch
    for k, part in enumerate(parts):
        owner = owner_of(k, count)
        rows_ref[owner, :span] = part[first : first + span]
        decode[owner, :count] = part[first + span : first + span + count].astype(F32)
    for h in range(count):
        for r in range(count):
            placed[h, r : r + 1, :] = decode[r, h : h + 1, :]
        rows_ref[h, span : span + count] = placed[h, :count].astype(BF16)
    total = None
    for h in range(count):
        term = jnp.dot(rows_ref[h], weights[h], preferred_element_type=F32)
        term = term.astype(BF16).astype(F32)
        total = term if total is None else total + term
    return total[: span + count].astype(BF16)


def first_output_kernel(count, span, *refs):
    parts = refs[:count]
    weights, first_new, early, late, out_ref, one_ref, two_ref = refs[count : count + 7]
    section = lax.axis_index("section")
    sections = lax.axis_size("section")
    out_ref[...] = summed_terms(count, span, 0, parts, weights, refs[count + 7 :])
    fresh = (first_new[...].astype(F32) + out_ref[...].astype(F32)).astype(BF16)
    is_last = section == sections - 1
    one_ref[...] = jnp.where(is_last, early[...], fresh)
    two_ref[...] = jnp.where(
        section == sections - 2, late[...], jnp.where(is_last, early[...], fresh)
    )


def second_output_kernel(count, span, *refs):
    parts = refs[:count]
    weights, first_new, pend_first, second_new = refs[count : count + 4]
    out_ref, hist_stream, hist_pend = refs[count + 4 : count + 7]
    scratch = refs[count + 7 : -1]
    sems = refs[-1]
    copies = [
        pltpu.make_async_copy(first_new, hist_stream.at[0], sems.at[0]),
        pltpu.make_async_copy(second_new, hist_stream.at[1], sems.at[1]),
        pltpu.make_async_copy(pend_first, hist_pend.at[0], sems.at[2]),
    ]
    for copy in copies:
        copy.start()
    out_ref[...] = summed_terms(count, span, span + count, parts, weights, scratch)
    last = pltpu.make_async_copy(out_ref, hist_pend.at[1], sems.at[3])
    last.start()
    for copy in copies:
        copy.wait()
    last.wait()


def third_output_kernel(count, span, *refs):
    parts = refs[:count]
    weights, third, pend_in = refs[count : count + 3]
    hist_stream, hist_pend = refs[count + 5 : count + 7]
    scratch = refs[count + 7 : -3]
    fresh, result, sems = refs[-3:]
    fresh[...] = (third[...].astype(F32) + pend_in[...].astype(F32)).astype(BF16)
    copy = pltpu.make_async_copy(fresh, hist_stream.at[2], sems.at[0])
    copy.start()
    result[...] = summed_terms(count, span, 0, parts, weights, scratch)
    last = pltpu.make_async_copy(result, hist_pend.at[2], sems.at[1])
    last.start()
    copy.wait()
    last.wait()


def fast_body(
    stream_in, pend_in, arrivals, norm_gain, wq, wkv, wo, cache, dec_len, span_seg
):
    count = lax.axis_size("tensor")
    rows, shard = stream_in.shape[1:]
    head = wq.shape[2]
    span = span_seg.shape[1]
    length = cache.shape[3]
    ticks = cache.shape[1]
    half = head // 2
    cached = cache.reshape(ticks, length, cache.shape[4])
    padded = (rows + 7) // 8 * 8
    message_rows = padded + count
    limit = pltpu.CompilerParams(vmem_limit_bytes=16 * 1024 * 1024)
    block = jax.ShapeDtypeStruct((rows, shard), BF16)
    history = jax.ShapeDtypeStruct((ticks, rows, shard), BF16)

    def cost(flops, moved_bytes):
        return pl.CostEstimate(
            flops=int(0 * flops), bytes_accessed=int(0 * moved_bytes), transcendentals=0
        )

    given = (norm_gain, wq[0], wkv[0], span_seg, dec_len.T, cached)
    pieces = (1, count, count, 1, 1, ticks)
    kept = pl.pallas_call(
        functools.partial(load_kernel, pieces),
        out_shape=tuple(jax.ShapeDtypeStruct(array.shape, array.dtype) for array in given),
        in_specs=[HBM] * len(given),
        out_specs=(VMEM,) * len(given),
        scratch_shapes=[pltpu.SemaphoreType.DMA((sum(pieces),))],
        compiler_params=limit,
        cost_estimate=cost(0, 4 * wq.shape[1] * 3 * head),
        name="load",
    )(*[in_hbm(array) for array in given])
    gain, wq_here, wkv_here, segments, lengths, cached = [in_vmem(array) for array in kept]

    def project(parts):
        batch = len(parts) // count
        return pl.pallas_call(
            functools.partial(project_kernel, count, span, batch),
            out_shape=(
                jax.ShapeDtypeStruct((batch, span, head), BF16),
                jax.ShapeDtypeStruct((batch * message_rows, 2 * head), BF16),
            ),
            in_specs=[VMEM] * (batch * count + 3),
            out_specs=(VMEM, VMEM),
            compiler_params=limit,
            cost_estimate=cost(
                2 * batch * rows * shard * count * 3 * head,
                2 * shard * count * (3 * head + rows),
            ),
            name="project",
        )(*[in_vmem(part) for part in parts], gain, wq_here, wkv_here)

    def attend(queries, parts, which):
        batch = len(which)
        return pl.pallas_call(
            functools.partial(attend_kernel, count, span, which),
            out_shape=jax.ShapeDtypeStruct((batch * (span + count), head), BF16),
            in_specs=[VMEM] * (count + 4),
            out_specs=VMEM,
            scratch_shapes=[
                pltpu.VMEM((2 * count, batch * message_rows, head), BF16),
                pltpu.VMEM((batch, 4, 8, head), F32),
            ],
            compiler_params=limit,
            cost_estimate=cost(
                batch * 4 * 8 * length * 4 * head,
                batch * (4 * length * 4 * head + count * message_rows * 4 * head),
            ),
            name="attend",
        )(queries, *[in_vmem(part) for part in parts], segments, lengths, cached)

    output_scratch = [
        pltpu.VMEM((count, padded, head), BF16),
        pltpu.VMEM((count, 8, head), F32),
        pltpu.VMEM((count, 8, head), F32),
    ]
    output_cost = cost(2 * rows * shard * count * head, 2 * shard * (count * head + rows))
    stream_parts = relayed_pieces_of(stream_in[0], "tensor")
    first_new = pl.pallas_call(
        begin_kernel,
        out_shape=block,
        in_specs=[VMEM] * 2,
        out_specs=VMEM,
        compiler_params=limit,
        cost_estimate=cost(0, 6 * rows * shard),
        name="begin",
    )(stream_in[0], pend_in[0])
    early, late = arrivals[0], arrivals[1]
    second = pl.pallas_call(
        choose_kernel,
        out_shape=block,
        in_specs=[VMEM] * 2,
        out_specs=VMEM,
        compiler_params=limit,
        cost_estimate=cost(0, 6 * rows * shard),
        name="choose",
    )(early, moved(first_new, "section", 1))
    second_parts = pieces_of(second, "tensor")
    queries, message = project(stream_parts + second_parts)
    message_parts = pieces_of(message, "tensor")
    small_block = jax.ShapeDtypeStruct((half, shard), BF16)
    cut = pl.pallas_call(
        functools.partial(cut_kernel, count),
        out_shape=(small_block,) * (count - 1),
        in_specs=[HBM],
        out_specs=(VMEM,) * (count - 1),
        scratch_shapes=[pltpu.SemaphoreType.DMA((count - 1,))],
        compiler_params=limit,
        cost_estimate=cost(0, 4 * half * shard * count),
        name="cut",
    )(in_hbm(wo[0]))
    blocks = [
        turned(cut[0], "tensor", 1),
        turned(cut[1], "tensor", 2),
        turned(cut[2], "tensor", 3),
    ]
    stacked = pl.pallas_call(
        stack_kernel,
        out_shape=jax.ShapeDtypeStruct((count - 1, half, shard), BF16),
        in_specs=[VMEM] * (count - 1),
        out_specs=VMEM,
        compiler_params=limit,
        cost_estimate=cost(0, 4 * half * shard * count),
        name="stack",
    )(*[in_vmem(block_k) for block_k in blocks])
    given = (in_hbm(wo[0]), *blocks, turned(stacked, "group", 1))
    weights = in_vmem(
        pl.pallas_call(
            functools.partial(place_kernel, count),
            out_shape=jax.ShapeDtypeStruct((count, head, shard), BF16),
            in_specs=[ANY] * len(given),
            out_specs=VMEM,
            scratch_shapes=[pltpu.SemaphoreType.DMA((2, count))],
            compiler_params=limit,
            cost_estimate=cost(0, 4 * count * head * shard),
            name="place",
        )(*given)
    )
    attended = attend(queries, message_parts, (0, 1))
    attended_parts = pieces_of(attended, "tensor")
    pend_first, one_on, two_on = pl.pallas_call(
        functools.partial(first_output_kernel, count, span),
        out_shape=(block, block, block),
        in_specs=[VMEM] * (count + 4),
        out_specs=(VMEM, VMEM, VMEM),
        scratch_shapes=output_scratch,
        compiler_params=limit,
        cost_estimate=output_cost,
        name="output_first",
    )(
        *[in_vmem(part) for part in attended_parts],
        weights,
        in_vmem(first_new),
        in_vmem(early),
        in_vmem(late),
    )
    third = turned(two_on, "section", 2)
    third_parts = pieces_of(third, "tensor")
    second_new = turned(one_on, "section", 1)
    pend_second, hist_stream, hist_pend = pl.pallas_call(
        functools.partial(second_output_kernel, count, span),
        out_shape=(block, history, history),
        in_specs=[VMEM] * (count + 4),
        out_specs=(VMEM, HBM, HBM),
        scratch_shapes=output_scratch + [pltpu.SemaphoreType.DMA((4,))],
        compiler_params=limit,
        cost_estimate=output_cost,
        name="output_second",
    )(
        *[in_vmem(part) for part in attended_parts],
        weights,
        in_vmem(first_new),
        in_vmem(pend_first),
        in_vmem(second_new),
    )
    pend_last_in = moved(pend_second, "section", 1)
    queries, message = project(third_parts)
    message_parts = pieces_of(message, "tensor")
    attended = attend(queries, message_parts, (2,))
    attended_parts = pieces_of(attended, "tensor")
    hist_stream, hist_pend = pl.pallas_call(
        functools.partial(third_output_kernel, count, span),
        out_shape=(history, history),
        in_specs=[VMEM] * (count + 3) + [HBM] * 2,
        out_specs=(HBM, HBM),
        scratch_shapes=output_scratch
        + [
            pltpu.VMEM((rows, shard), BF16),
            pltpu.VMEM((rows, shard), BF16),
            pltpu.SemaphoreType.DMA((2,)),
        ],
        input_output_aliases={count + 3: 0, count + 4: 1},
        compiler_params=limit,
        cost_estimate=output_cost,
        name="output_third",
    )(
        *[in_vmem(part) for part in attended_parts],
        weights,
        in_vmem(third),
        in_vmem(pend_last_in),
        hist_stream,
        hist_pend,
    )
    return hist_stream[None], hist_pend[None]


def passed_along(block, axis, distance):
    devices = range(lax.axis_size(axis))
    route = [(i - distance, i) for i in devices if i - distance in devices]
    return lax.ppermute(block, axis, route)


def rms_norm(stream, gain):
    values = stream.astype(jnp.float32)
    mean_sq = jnp.mean(values * values, axis=-1, keepdims=True)
    return (values * lax.rsqrt(mean_sq + EPS) * gain).astype(jnp.bfloat16)


def span_attention(queries, keys, values, segment):
    scale = 1.0 / math.sqrt(queries.shape[-1])
    scores = jnp.einsum("qd,kd->qk", queries, keys, preferred_element_type=jnp.float32) * scale
    count = segment.shape[0]
    rowsid = lax.broadcasted_iota(jnp.int32, (count, count), 0)
    colsid = lax.broadcasted_iota(jnp.int32, (count, count), 1)
    allowed = (segment[:, None] == segment[None, :]) & (colsid <= rowsid)
    scores = jnp.where(allowed, scores, NEG)
    top = jnp.max(scores, axis=-1, keepdims=True)
    expo = jnp.exp(scores - top)
    weights = (expo / jnp.sum(expo, axis=-1, keepdims=True)).astype(jnp.bfloat16)
    return jnp.dot(weights, values, preferred_element_type=jnp.float32).astype(jnp.bfloat16)


def decode_attention(queries, cache_keys, cache_values, new_keys, new_values, lengths):
    scale = 1.0 / math.sqrt(queries.shape[-1])
    scores = (
        jnp.einsum("rgjd,rcgd->rgjc", queries, cache_keys, preferred_element_type=jnp.float32)
        * scale
    )
    positions = lax.broadcasted_iota(jnp.int32, scores.shape, 3)
    scores = jnp.where(positions < lengths[:, None, None, None], scores, NEG)
    own = jnp.einsum("rgjd,rgd->rgj", queries, new_keys, preferred_element_type=jnp.float32) * scale
    top = jnp.maximum(jnp.max(scores, axis=-1), own)
    expo = jnp.exp(scores - top[..., None])
    own_expo = jnp.exp(own - top)
    total = jnp.sum(expo, axis=-1) + own_expo
    weights = (expo / total[..., None]).astype(jnp.bfloat16)
    own_weight = (own_expo / total).astype(jnp.bfloat16)
    result = jnp.einsum(
        "rgjc,rcgd->rgjd", weights, cache_values, preferred_element_type=jnp.float32
    )
    result = (
        result
        + own_weight.astype(jnp.float32)[..., None] * new_values.astype(jnp.float32)[:, :, None, :]
    )
    return result.astype(jnp.bfloat16)


def plain_body(stream_in, pend_in, arrivals, norm_gain, wq, wkv, wo, cache, dec_len, span_seg):
    tensor_count = lax.axis_size("tensor")
    section_count = lax.axis_size("section")
    tensor_index = lax.axis_index("tensor")
    section_index = lax.axis_index("section")
    row_count = stream_in.shape[1]
    shard = stream_in.shape[2]
    width = wq.shape[1]
    head_dim = wq.shape[2]
    kv_cols = cache.shape[4]
    kv_heads = kv_cols // (2 * head_dim)
    group_size = tensor_count // kv_heads
    span_rows = span_seg.shape[1]
    dec_rows = cache.shape[2]
    cache_len = cache.shape[3]
    tick_count = cache.shape[1]
    gain = norm_gain[0]
    kv_head = tensor_index // group_size
    stacked = jnp.concatenate([stream_in[0], pend_in[0], arrivals.reshape(-1, shard)], axis=0)
    gathered = lax.all_gather(stacked, "tensor", axis=1, tiled=True)
    stream = gathered[:row_count]
    pending = gathered[row_count : 2 * row_count]
    arrived = gathered[2 * row_count :].reshape(tick_count - 1, row_count, width)
    hist_stream = []
    hist_pend = []
    for tick in range(tick_count):
        micro = tick - section_index + section_count - 1
        lengths = lax.dynamic_index_in_dim(dec_len, micro, 0, keepdims=False)
        segment = lax.dynamic_index_in_dim(span_seg, micro, 0, keepdims=False)
        full_rows = stream
        normed = rms_norm(full_rows, gain)
        queries = jnp.dot(normed, wq[0], preferred_element_type=jnp.float32).astype(jnp.bfloat16)
        kv_part = jnp.dot(normed, wkv[0], preferred_element_type=jnp.float32).astype(jnp.bfloat16)
        keyval = lax.all_gather(kv_part, "tensor", axis=1, tiled=True)
        keys_all = keyval[:span_rows, : kv_heads * head_dim].reshape(span_rows, kv_heads, head_dim)
        values_all = keyval[:span_rows, kv_heads * head_dim :].reshape(
            span_rows, kv_heads, head_dim
        )
        own_keys = lax.dynamic_index_in_dim(keys_all, kv_head, 1, keepdims=False)
        own_values = lax.dynamic_index_in_dim(values_all, kv_head, 1, keepdims=False)
        span_out = span_attention(queries[:span_rows], own_keys, own_values, segment)
        dec_queries = queries[span_rows:].reshape(-1, 1, head_dim)
        row_queries = lax.all_to_all(dec_queries, "tensor", split_axis=0, concat_axis=1, tiled=True)
        row_queries = row_queries.reshape(dec_rows, kv_heads, group_size, head_dim)
        row_start = span_rows + tensor_index * dec_rows
        new_kv = lax.dynamic_slice_in_dim(keyval, row_start, dec_rows, 0)
        new_keys = new_kv[:, : kv_heads * head_dim].reshape(dec_rows, kv_heads, head_dim)
        new_values = new_kv[:, kv_heads * head_dim :].reshape(dec_rows, kv_heads, head_dim)
        cache_now = cache[0, tick]
        cache_keys = cache_now[:, :, : kv_heads * head_dim].reshape(
            dec_rows, cache_len, kv_heads, head_dim
        )
        cache_values = cache_now[:, :, kv_heads * head_dim :].reshape(
            dec_rows, cache_len, kv_heads, head_dim
        )
        row_out = decode_attention(
            row_queries, cache_keys, cache_values, new_keys, new_values, lengths
        )
        row_out = row_out.reshape(dec_rows, tensor_count, head_dim)
        dec_back = lax.all_to_all(
            row_out, "tensor", split_axis=1, concat_axis=0, tiled=True
        ).reshape(-1, head_dim)
        attended = jnp.concatenate([span_out, dec_back], axis=0)
        term = jnp.dot(attended, wo[0], preferred_element_type=jnp.float32).astype(jnp.bfloat16)
        pending_new = lax.psum(term, "tensor").astype(jnp.float32).astype(jnp.bfloat16)
        stream_new = (stream.astype(jnp.float32) + pending.astype(jnp.float32)).astype(jnp.bfloat16)
        hist_stream.append(lax.dynamic_slice_in_dim(stream_new, tensor_index * shard, shard, 1))
        hist_pend.append(lax.dynamic_slice_in_dim(pending_new, tensor_index * shard, shard, 1))
        if tick + 1 < tick_count:
            moved_stream, moved_pend = passed_along((stream_new, pending_new), "section", 1)
            first_section = section_index == 0
            stream = jnp.where(first_section, arrived[tick], moved_stream)
            pending = jnp.where(first_section, jnp.zeros_like(moved_pend), moved_pend)
    return (jnp.stack(hist_stream)[None], jnp.stack(hist_pend)[None])


def body(stream_in, pend_in, arrivals, norm_gain, wq, wkv, wo, cache, dec_len, span_seg):
    count = lax.axis_size("tensor")
    head = wq.shape[2]
    fits = (
        head == 128
        and lax.axis_size("group") == 2
        and count <= 8
        and cache.shape[1] == 3
        and cache.shape[2] == 1
        and cache.shape[4] == 2 * head * count
        and wkv.shape[2] == 2 * head
        and stream_in.shape[2] % 128 == 0
        and span_seg.shape[1] % 16 == 0
        and stream_in.shape[1] == span_seg.shape[1] + count
    )
    chosen = fast_body if fits else plain_body
    return chosen(
        stream_in, pend_in, arrivals, norm_gain, wq, wkv, wo, cache, dec_len, span_seg
    )


def solution(mesh):
    return jax.shard_map(
        body,
        mesh=mesh,
        in_specs=(
            P("section", "group", "tensor"),
            P("section", "group", "tensor"),
            P(None, "group", "tensor"),
            P("section", None),
            P("section", None, "tensor"),
            P("section", None, "tensor"),
            P("section", "tensor", None),
            P("section", "group", "tensor", None, None),
            P("group", "tensor"),
            P("group", None),
        ),
        out_specs=(P("section", None, "group", "tensor"), P("section", None, "group", "tensor")),
        check_vma=False,
    )
```

```python
import functools
import math

import jax
import jax.numpy as jnp
from jax import lax
from jax.experimental import pallas as pl
from jax.experimental.pallas import tpu as pltpu
from jax.sharding import PartitionSpec as P

EPS = 1e-05
NEG = -1e30
BF16 = jnp.bfloat16
F32 = jnp.float32


def moved(block, axis, distance):
    devices = range(lax.axis_size(axis))
    route = [(i - distance, i) for i in devices if i - distance in devices]
    return lax.ppermute(block, axis, route)


def turned(block, axis, distance):
    count = lax.axis_size(axis)
    return lax.ppermute(block, axis, [(i, (i + distance) % count) for i in range(count)])


def pieces_of(block, axis):
    return [block] + [turned(block, axis, k) for k in range(1, lax.axis_size(axis))]


def relayed_pieces_of(block, axis):
    if lax.axis_size(axis) != 4:
        return pieces_of(block, axis)
    one = turned(block, axis, 1)
    three = turned(block, axis, 3)
    return [block, one, turned(one, axis, 1), three]


VMEM = pl.BlockSpec(memory_space=pltpu.VMEM)
HBM = pl.BlockSpec(memory_space=pltpu.HBM)
ANY = pl.BlockSpec(memory_space=pl.ANY)


def in_hbm(array):
    return pltpu.with_memory_space_constraint(array, pltpu.HBM)


def in_vmem(array):
    return pltpu.with_memory_space_constraint(array, pltpu.VMEM)


def owner_of(k, count):
    return lax.rem(lax.axis_index("tensor") - k + count, count)


def load_kernel(pieces, *refs):
    given, kept, sems = refs[: len(pieces)], refs[len(pieces) : -1], refs[-1]
    copies = []
    for source, target, count in zip(given, kept, pieces):
        rows = source.shape[0] // count
        for k in range(count):
            part = pl.ds(k * rows, rows)
            copies.append(
                pltpu.make_async_copy(source.at[part], target.at[part], sems.at[len(copies)])
            )
    for copy in copies:
        copy.start()
    for copy in copies:
        copy.wait()


def begin_kernel(stream_ref, pend_ref, out_ref):
    out_ref[...] = (stream_ref[...].astype(F32) + pend_ref[...].astype(F32)).astype(BF16)


def choose_kernel(arrived_ref, moved_ref, out_ref):
    out_ref[...] = jnp.where(
        lax.axis_index("section") == 0, arrived_ref[...], moved_ref[...]
    )


def cut_kernel(count, wo_ref, *refs):
    blocks, sems = refs[:-1], refs[-1]
    half, shard = blocks[0].shape
    rows = pl.ds(pl.multiple_of(lax.axis_index("group") * half, half), half)
    copies = []
    for k in range(1, count):
        target = lax.rem(lax.axis_index("tensor") + k, count)
        columns = pl.ds(pl.multiple_of(target * shard, shard), shard)
        copies.append(
            pltpu.make_async_copy(wo_ref.at[rows, columns], blocks[k - 1], sems.at[k - 1])
        )
    for copy in copies:
        copy.start()
    for copy in copies:
        copy.wait()


def stack_kernel(*refs):
    out_ref = refs[-1]
    for k, block in enumerate(refs[:-1]):
        out_ref[k] = block[...]


def place_kernel(count, *refs):
    wo_ref = refs[0]
    got = refs[1:count]
    other_ref, weights, sems = refs[count:]
    me, half_index = lax.axis_index("tensor"), lax.axis_index("group")
    half, shard = got[0].shape
    begin = pl.multiple_of(half_index * half, half)
    rest = pl.multiple_of(half - half_index * half, half)
    columns = pl.ds(pl.multiple_of(me * shard, shard), shard)
    copies = [pltpu.make_async_copy(wo_ref.at[:, columns], weights.at[me], sems.at[0, 0])]
    for k in range(1, count):
        owner = owner_of(k, count)
        copies.append(
            pltpu.make_async_copy(
                got[k - 1], weights.at[owner, pl.ds(begin, half)], sems.at[0, k]
            )
        )
        copies.append(
            pltpu.make_async_copy(
                other_ref.at[k - 1], weights.at[owner, pl.ds(rest, half)], sems.at[1, k]
            )
        )
    for copy in copies:
        copy.start()
    for copy in copies:
        copy.wait()


def project_kernel(count, span, batch, *refs):
    parts = refs[: batch * count]
    gain_ref, wq_ref, wkv_ref, query_ref, same_ref, other_ref = refs[batch * count :]
    odd = lax.rem(lax.axis_index("tensor"), 2) == 1
    head = wq_ref.shape[1]
    rows, shard = parts[0].shape
    block = same_ref.shape[0] // batch
    for b in range(batch):
        own = parts[b * count : (b + 1) * count]
        total = jnp.zeros((rows, 1), F32)
        for part in own:
            values = part[...].astype(F32)
            total = total + jnp.sum(values * values, axis=-1, keepdims=True)
        scale = lax.rsqrt(total / (shard * count) + EPS)
        queries = jnp.zeros((rows, wq_ref.shape[1]), F32)
        keyval = jnp.zeros((rows, wkv_ref.shape[1]), F32)
        for k, part in enumerate(own):
            here = pl.ds(pl.multiple_of(owner_of(k, count) * shard, shard), shard)
            normed = (part[...].astype(F32) * scale * gain_ref[:, here]).astype(BF16)
            queries = queries + jnp.dot(normed, wq_ref[here, :], preferred_element_type=F32)
            keyval = keyval + jnp.dot(normed, wkv_ref[here, :], preferred_element_type=F32)
        queries = queries.astype(BF16)
        query_ref[b] = queries[:span]
        even_half, odd_half = keyval[:, :head], keyval[:, head:]
        for message_ref, is_odd in ((same_ref, odd), (other_ref, jnp.logical_not(odd))):
            message_ref[b * block : b * block + span] = jnp.where(
                is_odd, odd_half[:span], even_half[:span]
            ).astype(BF16)
            for n, rest in enumerate((even_half, odd_half, queries)):
                first = b * block + span + 8 * n
                message_ref[first : first + rows - span] = rest[span:].astype(BF16)


def attend_kernel(count, span, ticks, *refs):
    query_ref = refs[0]
    parts = refs[1 : 1 + count]
    segment_ref, length_ref, cache_ref, out_ref, blocks, small = refs[1 + count :]
    me = lax.axis_index("tensor")
    head = query_ref.shape[2]
    factor = 1.0 / math.sqrt(head)
    heads = count
    block = parts[0].shape[0] // len(ticks)
    for k, part in enumerate(parts):
        blocks[owner_of(k, count)] = part[...]
    small[...] = jnp.zeros_like(small)
    row_ids = lax.broadcasted_iota(jnp.int32, (span, span), 0)
    col_ids = lax.broadcasted_iota(jnp.int32, (span, span), 1)
    picked = lax.broadcasted_iota(jnp.int32, (count, head), 0) == me

    def own_row(rows):
        return jnp.sum(jnp.where(picked, rows.astype(F32), 0.0), axis=0, keepdims=True)

    for b, tick in enumerate(ticks):
        micro = tick - lax.axis_index("section") + lax.axis_size("section") - 1
        first = b * block
        out = b * (span + count)
        keys = blocks[lax.div(me, 2), first : first + span]
        values = blocks[heads // 2 + lax.div(me, 2), first : first + span]
        scores = (
            lax.dot_general(
                query_ref[b], keys, (((1,), (1,)), ((), ())), preferred_element_type=F32
            )
            * factor
        )
        across = segment_ref[pl.ds(micro, 1), :]
        down = jnp.sum(jnp.where(row_ids == col_ids, across, 0), axis=1, keepdims=True)
        scores = jnp.where((down == across) & (col_ids <= row_ids), scores, NEG)
        expo = jnp.exp(scores - jnp.max(scores, axis=-1, keepdims=True))
        weights = (expo / jnp.sum(expo, axis=-1, keepdims=True)).astype(BF16)
        out_ref[out : out + span] = jnp.dot(
            weights, values, preferred_element_type=F32
        ).astype(BF16)

        def new_row(device, n):
            start = first + span + 8 * n
            return own_row(blocks[device, start : start + count])

        for h in range(heads):
            small[b, 0, h : h + 1, :] = new_row(h, 2)
            small[b, 1, h : h + 1, :] = new_row(h // 2, h % 2)
            small[b, 2, h : h + 1, :] = new_row((heads + h) // 2, h % 2)
        queries = small[b, 0]
        line = lax.broadcasted_iota(jnp.int32, queries.shape, 0)
        spread = jnp.concatenate(
            [jnp.where(line == h, queries, 0.0) for h in range(heads)], axis=1
        ).astype(BF16)
        own = jnp.sum(queries * small[b, 1], axis=-1, keepdims=True) * factor
        dec_scores = (
            lax.dot_general(
                spread,
                cache_ref[tick, :, : heads * head],
                (((1,), (1,)), ((), ())),
                preferred_element_type=F32,
            )
            * factor
        )
        positions = lax.broadcasted_iota(jnp.int32, dec_scores.shape, 1)
        lanes = lax.broadcasted_iota(jnp.int32, length_ref.shape, 1)
        live = jnp.sum(jnp.where(lanes == micro, length_ref[...], 0), axis=1, keepdims=True)
        dec_scores = jnp.where(positions < live, dec_scores, NEG)
        top = jnp.maximum(jnp.max(dec_scores, axis=-1, keepdims=True), own)
        dec_expo = jnp.exp(dec_scores - top)
        own_expo = jnp.exp(own - top)
        total = jnp.sum(dec_expo, axis=-1, keepdims=True) + own_expo
        dec_weights = (dec_expo / total).astype(BF16)
        own_weight = (own_expo / total).astype(BF16).astype(F32)
        result = jnp.dot(dec_weights, cache_ref[tick, :, heads * head :], preferred_element_type=F32)
        extra = own_weight * small[b, 2]
        for h in range(heads):
            row = result[h : h + 1, h * head : (h + 1) * head] + extra[h : h + 1]
            small[b, 3, h : h + 1, :] = row
        out_ref[out + span : out + span + count] = small[b, 3, :heads].astype(BF16)


def summed_terms(count, span, first, parts, weights, scratch):
    rows_ref, decode, placed = scratch
    for k, part in enumerate(parts):
        owner = owner_of(k, count)
        rows_ref[owner, :span] = part[first : first + span]
        decode[owner, :count] = part[first + span : first + span + count].astype(F32)
    for h in range(count):
        for r in range(count):
            placed[h, r : r + 1, :] = decode[r, h : h + 1, :]
        rows_ref[h, span : span + count] = placed[h, :count].astype(BF16)
    total = None
    for h in range(count):
        term = jnp.dot(rows_ref[h], weights[h], preferred_element_type=F32)
        term = term.astype(BF16).astype(F32)
        total = term if total is None else total + term
    return total[: span + count].astype(BF16)


def first_output_kernel(count, span, *refs):
    parts = refs[:count]
    weights, first_new, early, late, out_ref, one_ref, two_ref = refs[count : count + 7]
    section = lax.axis_index("section")
    sections = lax.axis_size("section")
    out_ref[...] = summed_terms(count, span, 0, parts, weights, refs[count + 7 :])
    fresh = (first_new[...].astype(F32) + out_ref[...].astype(F32)).astype(BF16)
    is_last = section == sections - 1
    one_ref[...] = jnp.where(is_last, early[...], fresh)
    two_ref[...] = jnp.where(
        section == sections - 2, late[...], jnp.where(is_last, early[...], fresh)
    )


def second_output_kernel(count, span, *refs):
    parts = refs[:count]
    weights, first_new, pend_first, second_new = refs[count : count + 4]
    out_ref, hist_stream, hist_pend = refs[count + 4 : count + 7]
    scratch = refs[count + 7 : -1]
    sems = refs[-1]
    copies = [
        pltpu.make_async_copy(first_new, hist_stream.at[0], sems.at[0]),
        pltpu.make_async_copy(second_new, hist_stream.at[1], sems.at[1]),
        pltpu.make_async_copy(pend_first, hist_pend.at[0], sems.at[2]),
    ]
    for copy in copies:
        copy.start()
    out_ref[...] = summed_terms(count, span, span + count, parts, weights, scratch)
    last = pltpu.make_async_copy(out_ref, hist_pend.at[1], sems.at[3])
    last.start()
    for copy in copies:
        copy.wait()
    last.wait()


def third_output_kernel(count, span, *refs):
    parts = refs[:count]
    weights, third, pend_in = refs[count : count + 3]
    hist_stream, hist_pend = refs[count + 5 : count + 7]
    scratch = refs[count + 7 : -3]
    fresh, result, sems = refs[-3:]
    fresh[...] = (third[...].astype(F32) + pend_in[...].astype(F32)).astype(BF16)
    copy = pltpu.make_async_copy(fresh, hist_stream.at[2], sems.at[0])
    copy.start()
    result[...] = summed_terms(count, span, 0, parts, weights, scratch)
    last = pltpu.make_async_copy(result, hist_pend.at[2], sems.at[1])
    last.start()
    copy.wait()
    last.wait()


def fast_body(
    stream_in, pend_in, arrivals, norm_gain, wq, wkv, wo, cache, dec_len, span_seg
):
    count = lax.axis_size("tensor")
    rows, shard = stream_in.shape[1:]
    head = wq.shape[2]
    span = span_seg.shape[1]
    length = cache.shape[3]
    ticks = cache.shape[1]
    half = head // 2
    cached = cache.reshape(ticks, length, cache.shape[4])
    padded = (rows + 7) // 8 * 8
    message_rows = span + 24
    limit = pltpu.CompilerParams(vmem_limit_bytes=16 * 1024 * 1024)
    block = jax.ShapeDtypeStruct((rows, shard), BF16)
    history = jax.ShapeDtypeStruct((ticks, rows, shard), BF16)

    def cost(flops, moved_bytes):
        return pl.CostEstimate(
            flops=int(0 * flops), bytes_accessed=int(0 * moved_bytes), transcendentals=0
        )

    given = (norm_gain, wq[0], wkv[0], span_seg, dec_len.T, cached)
    pieces = (1, count, count, 1, 1, ticks)
    kept = pl.pallas_call(
        functools.partial(load_kernel, pieces),
        out_shape=tuple(jax.ShapeDtypeStruct(array.shape, array.dtype) for array in given),
        in_specs=[HBM] * len(given),
        out_specs=(VMEM,) * len(given),
        scratch_shapes=[pltpu.SemaphoreType.DMA((sum(pieces),))],
        compiler_params=limit,
        cost_estimate=cost(0, 4 * wq.shape[1] * 3 * head),
        name="load",
    )(*[in_hbm(array) for array in given])
    gain, wq_here, wkv_here, segments, lengths, cached = [in_vmem(array) for array in kept]

    def project(parts):
        batch = len(parts) // count
        return pl.pallas_call(
            functools.partial(project_kernel, count, span, batch),
            out_shape=(
                jax.ShapeDtypeStruct((batch, span, head), BF16),
                jax.ShapeDtypeStruct((batch * message_rows, head), BF16),
                jax.ShapeDtypeStruct((batch * message_rows, head), BF16),
            ),
            in_specs=[VMEM] * (batch * count + 3),
            out_specs=(VMEM, VMEM, VMEM),
            compiler_params=limit,
            cost_estimate=cost(
                2 * batch * rows * shard * count * 3 * head,
                2 * shard * count * (3 * head + rows),
            ),
            name="project",
        )(*[in_vmem(part) for part in parts], gain, wq_here, wkv_here)

    def attend(queries, parts, which):
        batch = len(which)
        return pl.pallas_call(
            functools.partial(attend_kernel, count, span, which),
            out_shape=jax.ShapeDtypeStruct((batch * (span + count), head), BF16),
            in_specs=[VMEM] * (count + 4),
            out_specs=VMEM,
            scratch_shapes=[
                pltpu.VMEM((count, batch * message_rows, head), BF16),
                pltpu.VMEM((batch, 4, 8, head), F32),
            ],
            compiler_params=limit,
            cost_estimate=cost(
                batch * 4 * 8 * length * 4 * head,
                batch * (4 * length * 4 * head + count * message_rows * 4 * head),
            ),
            name="attend",
        )(queries, *[in_vmem(part) for part in parts], segments, lengths, cached)

    def message_pieces(same, other):
        kinds = [same if k % 2 == 0 else other for k in range(count)]
        return [same] + [turned(kinds[k], "tensor", k) for k in range(1, count)]

    output_scratch = [
        pltpu.VMEM((count, padded, head), BF16),
        pltpu.VMEM((count, 8, head), F32),
        pltpu.VMEM((count, 8, head), F32),
    ]
    output_cost = cost(2 * rows * shard * count * head, 2 * shard * (count * head + rows))
    stream_parts = relayed_pieces_of(stream_in[0], "tensor")
    first_new = pl.pallas_call(
        begin_kernel,
        out_shape=block,
        in_specs=[VMEM] * 2,
        out_specs=VMEM,
        compiler_params=limit,
        cost_estimate=cost(0, 6 * rows * shard),
        name="begin",
    )(stream_in[0], pend_in[0])
    early, late = arrivals[0], arrivals[1]
    second = pl.pallas_call(
        choose_kernel,
        out_shape=block,
        in_specs=[VMEM] * 2,
        out_specs=VMEM,
        compiler_params=limit,
        cost_estimate=cost(0, 6 * rows * shard),
        name="choose",
    )(early, moved(first_new, "section", 1))
    second_parts = pieces_of(second, "tensor")
    queries, same, other_half = project(stream_parts + second_parts)
    message_parts = message_pieces(same, other_half)
    small_block = jax.ShapeDtypeStruct((half, shard), BF16)
    cut = pl.pallas_call(
        functools.partial(cut_kernel, count),
        out_shape=(small_block,) * (count - 1),
        in_specs=[HBM],
        out_specs=(VMEM,) * (count - 1),
        scratch_shapes=[pltpu.SemaphoreType.DMA((count - 1,))],
        compiler_params=limit,
        cost_estimate=cost(0, 4 * half * shard * count),
        name="cut",
    )(in_hbm(wo[0]))
    blocks = [
        turned(cut[0], "tensor", 1),
        turned(cut[1], "tensor", 2),
        turned(cut[2], "tensor", 3),
    ]
    stacked = pl.pallas_call(
        stack_kernel,
        out_shape=jax.ShapeDtypeStruct((count - 1, half, shard), BF16),
        in_specs=[VMEM] * (count - 1),
        out_specs=VMEM,
        compiler_params=limit,
        cost_estimate=cost(0, 4 * half * shard * count),
        name="stack",
    )(*[in_vmem(block_k) for block_k in blocks])
    given = (in_hbm(wo[0]), *blocks, turned(stacked, "group", 1))
    weights = in_vmem(
        pl.pallas_call(
            functools.partial(place_kernel, count),
            out_shape=jax.ShapeDtypeStruct((count, head, shard), BF16),
            in_specs=[ANY] * len(given),
            out_specs=VMEM,
            scratch_shapes=[pltpu.SemaphoreType.DMA((2, count))],
            compiler_params=limit,
            cost_estimate=cost(0, 4 * count * head * shard),
            name="place",
        )(*given)
    )
    attended = attend(queries, message_parts, (0, 1))
    attended_parts = pieces_of(attended, "tensor")
    pend_first, one_on, two_on = pl.pallas_call(
        functools.partial(first_output_kernel, count, span),
        out_shape=(block, block, block),
        in_specs=[VMEM] * (count + 4),
        out_specs=(VMEM, VMEM, VMEM),
        scratch_shapes=output_scratch,
        compiler_params=limit,
        cost_estimate=output_cost,
        name="output_first",
    )(
        *[in_vmem(part) for part in attended_parts],
        weights,
        in_vmem(first_new),
        in_vmem(early),
        in_vmem(late),
    )
    third = turned(two_on, "section", 2)
    third_parts = pieces_of(third, "tensor")
    second_new = turned(one_on, "section", 1)
    pend_second, hist_stream, hist_pend = pl.pallas_call(
        functools.partial(second_output_kernel, count, span),
        out_shape=(block, history, history),
        in_specs=[VMEM] * (count + 4),
        out_specs=(VMEM, HBM, HBM),
        scratch_shapes=output_scratch + [pltpu.SemaphoreType.DMA((4,))],
        compiler_params=limit,
        cost_estimate=output_cost,
        name="output_second",
    )(
        *[in_vmem(part) for part in attended_parts],
        weights,
        in_vmem(first_new),
        in_vmem(pend_first),
        in_vmem(second_new),
    )
    pend_last_in = moved(pend_second, "section", 1)
    queries, same, other_half = project(third_parts)
    message_parts = message_pieces(same, other_half)
    attended = attend(queries, message_parts, (2,))
    attended_parts = pieces_of(attended, "tensor")
    hist_stream, hist_pend = pl.pallas_call(
        functools.partial(third_output_kernel, count, span),
        out_shape=(history, history),
        in_specs=[VMEM] * (count + 3) + [HBM] * 2,
        out_specs=(HBM, HBM),
        scratch_shapes=output_scratch
        + [
            pltpu.VMEM((rows, shard), BF16),
            pltpu.VMEM((rows, shard), BF16),
            pltpu.SemaphoreType.DMA((2,)),
        ],
        input_output_aliases={count + 3: 0, count + 4: 1},
        compiler_params=limit,
        cost_estimate=output_cost,
        name="output_third",
    )(
        *[in_vmem(part) for part in attended_parts],
        weights,
        in_vmem(third),
        in_vmem(pend_last_in),
        hist_stream,
        hist_pend,
    )
    return hist_stream[None], hist_pend[None]


def passed_along(block, axis, distance):
    devices = range(lax.axis_size(axis))
    route = [(i - distance, i) for i in devices if i - distance in devices]
    return lax.ppermute(block, axis, route)


def rms_norm(stream, gain):
    values = stream.astype(jnp.float32)
    mean_sq = jnp.mean(values * values, axis=-1, keepdims=True)
    return (values * lax.rsqrt(mean_sq + EPS) * gain).astype(jnp.bfloat16)


def span_attention(queries, keys, values, segment):
    scale = 1.0 / math.sqrt(queries.shape[-1])
    scores = jnp.einsum("qd,kd->qk", queries, keys, preferred_element_type=jnp.float32) * scale
    count = segment.shape[0]
    rowsid = lax.broadcasted_iota(jnp.int32, (count, count), 0)
    colsid = lax.broadcasted_iota(jnp.int32, (count, count), 1)
    allowed = (segment[:, None] == segment[None, :]) & (colsid <= rowsid)
    scores = jnp.where(allowed, scores, NEG)
    top = jnp.max(scores, axis=-1, keepdims=True)
    expo = jnp.exp(scores - top)
    weights = (expo / jnp.sum(expo, axis=-1, keepdims=True)).astype(jnp.bfloat16)
    return jnp.dot(weights, values, preferred_element_type=jnp.float32).astype(jnp.bfloat16)


def decode_attention(queries, cache_keys, cache_values, new_keys, new_values, lengths):
    scale = 1.0 / math.sqrt(queries.shape[-1])
    scores = (
        jnp.einsum("rgjd,rcgd->rgjc", queries, cache_keys, preferred_element_type=jnp.float32)
        * scale
    )
    positions = lax.broadcasted_iota(jnp.int32, scores.shape, 3)
    scores = jnp.where(positions < lengths[:, None, None, None], scores, NEG)
    own = jnp.einsum("rgjd,rgd->rgj", queries, new_keys, preferred_element_type=jnp.float32) * scale
    top = jnp.maximum(jnp.max(scores, axis=-1), own)
    expo = jnp.exp(scores - top[..., None])
    own_expo = jnp.exp(own - top)
    total = jnp.sum(expo, axis=-1) + own_expo
    weights = (expo / total[..., None]).astype(jnp.bfloat16)
    own_weight = (own_expo / total).astype(jnp.bfloat16)
    result = jnp.einsum(
        "rgjc,rcgd->rgjd", weights, cache_values, preferred_element_type=jnp.float32
    )
    result = (
        result
        + own_weight.astype(jnp.float32)[..., None] * new_values.astype(jnp.float32)[:, :, None, :]
    )
    return result.astype(jnp.bfloat16)


def plain_body(stream_in, pend_in, arrivals, norm_gain, wq, wkv, wo, cache, dec_len, span_seg):
    tensor_count = lax.axis_size("tensor")
    section_count = lax.axis_size("section")
    tensor_index = lax.axis_index("tensor")
    section_index = lax.axis_index("section")
    row_count = stream_in.shape[1]
    shard = stream_in.shape[2]
    width = wq.shape[1]
    head_dim = wq.shape[2]
    kv_cols = cache.shape[4]
    kv_heads = kv_cols // (2 * head_dim)
    group_size = tensor_count // kv_heads
    span_rows = span_seg.shape[1]
    dec_rows = cache.shape[2]
    cache_len = cache.shape[3]
    tick_count = cache.shape[1]
    gain = norm_gain[0]
    kv_head = tensor_index // group_size
    stacked = jnp.concatenate([stream_in[0], pend_in[0], arrivals.reshape(-1, shard)], axis=0)
    gathered = lax.all_gather(stacked, "tensor", axis=1, tiled=True)
    stream = gathered[:row_count]
    pending = gathered[row_count : 2 * row_count]
    arrived = gathered[2 * row_count :].reshape(tick_count - 1, row_count, width)
    hist_stream = []
    hist_pend = []
    for tick in range(tick_count):
        micro = tick - section_index + section_count - 1
        lengths = lax.dynamic_index_in_dim(dec_len, micro, 0, keepdims=False)
        segment = lax.dynamic_index_in_dim(span_seg, micro, 0, keepdims=False)
        full_rows = stream
        normed = rms_norm(full_rows, gain)
        queries = jnp.dot(normed, wq[0], preferred_element_type=jnp.float32).astype(jnp.bfloat16)
        kv_part = jnp.dot(normed, wkv[0], preferred_element_type=jnp.float32).astype(jnp.bfloat16)
        keyval = lax.all_gather(kv_part, "tensor", axis=1, tiled=True)
        keys_all = keyval[:span_rows, : kv_heads * head_dim].reshape(span_rows, kv_heads, head_dim)
        values_all = keyval[:span_rows, kv_heads * head_dim :].reshape(
            span_rows, kv_heads, head_dim
        )
        own_keys = lax.dynamic_index_in_dim(keys_all, kv_head, 1, keepdims=False)
        own_values = lax.dynamic_index_in_dim(values_all, kv_head, 1, keepdims=False)
        span_out = span_attention(queries[:span_rows], own_keys, own_values, segment)
        dec_queries = queries[span_rows:].reshape(-1, 1, head_dim)
        row_queries = lax.all_to_all(dec_queries, "tensor", split_axis=0, concat_axis=1, tiled=True)
        row_queries = row_queries.reshape(dec_rows, kv_heads, group_size, head_dim)
        row_start = span_rows + tensor_index * dec_rows
        new_kv = lax.dynamic_slice_in_dim(keyval, row_start, dec_rows, 0)
        new_keys = new_kv[:, : kv_heads * head_dim].reshape(dec_rows, kv_heads, head_dim)
        new_values = new_kv[:, kv_heads * head_dim :].reshape(dec_rows, kv_heads, head_dim)
        cache_now = cache[0, tick]
        cache_keys = cache_now[:, :, : kv_heads * head_dim].reshape(
            dec_rows, cache_len, kv_heads, head_dim
        )
        cache_values = cache_now[:, :, kv_heads * head_dim :].reshape(
            dec_rows, cache_len, kv_heads, head_dim
        )
        row_out = decode_attention(
            row_queries, cache_keys, cache_values, new_keys, new_values, lengths
        )
        row_out = row_out.reshape(dec_rows, tensor_count, head_dim)
        dec_back = lax.all_to_all(
            row_out, "tensor", split_axis=1, concat_axis=0, tiled=True
        ).reshape(-1, head_dim)
        attended = jnp.concatenate([span_out, dec_back], axis=0)
        term = jnp.dot(attended, wo[0], preferred_element_type=jnp.float32).astype(jnp.bfloat16)
        pending_new = lax.psum(term, "tensor").astype(jnp.float32).astype(jnp.bfloat16)
        stream_new = (stream.astype(jnp.float32) + pending.astype(jnp.float32)).astype(jnp.bfloat16)
        hist_stream.append(lax.dynamic_slice_in_dim(stream_new, tensor_index * shard, shard, 1))
        hist_pend.append(lax.dynamic_slice_in_dim(pending_new, tensor_index * shard, shard, 1))
        if tick + 1 < tick_count:
            moved_stream, moved_pend = passed_along((stream_new, pending_new), "section", 1)
            first_section = section_index == 0
            stream = jnp.where(first_section, arrived[tick], moved_stream)
            pending = jnp.where(first_section, jnp.zeros_like(moved_pend), moved_pend)
    return (jnp.stack(hist_stream)[None], jnp.stack(hist_pend)[None])


def body(stream_in, pend_in, arrivals, norm_gain, wq, wkv, wo, cache, dec_len, span_seg):
    count = lax.axis_size("tensor")
    head = wq.shape[2]
    fits = (
        head == 128
        and lax.axis_size("group") == 2
        and cache.shape[1] == 3
        and cache.shape[2] == 1
        and cache.shape[4] == 2 * head * count
        and wkv.shape[2] == 2 * head
        and stream_in.shape[2] % 128 == 0
        and span_seg.shape[1] % 16 == 0
        and stream_in.shape[1] == span_seg.shape[1] + count
        and count == 4
    )
    chosen = fast_body if fits else plain_body
    return chosen(
        stream_in, pend_in, arrivals, norm_gain, wq, wkv, wo, cache, dec_len, span_seg
    )


def solution(mesh):
    return jax.shard_map(
        body,
        mesh=mesh,
        in_specs=(
            P("section", "group", "tensor"),
            P("section", "group", "tensor"),
            P(None, "group", "tensor"),
            P("section", None),
            P("section", None, "tensor"),
            P("section", None, "tensor"),
            P("section", "tensor", None),
            P("section", "group", "tensor", None, None),
            P("group", "tensor"),
            P("group", None),
        ),
        out_specs=(P("section", None, "group", "tensor"), P("section", None, "group", "tensor")),
        check_vma=False,
    )
```

```python
import functools
import math

import jax
import jax.numpy as jnp
from jax import lax
from jax.experimental import pallas as pl
from jax.experimental.pallas import tpu as pltpu
from jax.sharding import PartitionSpec as P

EPS = 1e-05
NEG = -1e30
BF16 = jnp.bfloat16
F32 = jnp.float32


def moved(block, axis, distance):
    devices = range(lax.axis_size(axis))
    route = [(i - distance, i) for i in devices if i - distance in devices]
    return lax.ppermute(block, axis, route)


def turned(block, axis, distance):
    count = lax.axis_size(axis)
    return lax.ppermute(block, axis, [(i, (i + distance) % count) for i in range(count)])


def pieces_of(block, axis):
    return [block] + [turned(block, axis, k) for k in range(1, lax.axis_size(axis))]


def relayed_pieces_of(block, axis):
    if lax.axis_size(axis) != 4:
        return pieces_of(block, axis)
    one = turned(block, axis, 1)
    three = turned(block, axis, 3)
    return [block, one, turned(one, axis, 1), three]


VMEM = pl.BlockSpec(memory_space=pltpu.VMEM)
HBM = pl.BlockSpec(memory_space=pltpu.HBM)
ANY = pl.BlockSpec(memory_space=pl.ANY)


def in_hbm(array):
    return pltpu.with_memory_space_constraint(array, pltpu.HBM)


def in_vmem(array):
    return pltpu.with_memory_space_constraint(array, pltpu.VMEM)


def owner_of(k, count):
    return lax.rem(lax.axis_index("tensor") - k + count, count)


def load_kernel(pieces, *refs):
    given, kept, sems = refs[: len(pieces)], refs[len(pieces) : -1], refs[-1]
    copies = []
    for source, target, count in zip(given, kept, pieces):
        rows = source.shape[0] // count
        for k in range(count):
            part = pl.ds(k * rows, rows)
            copies.append(
                pltpu.make_async_copy(source.at[part], target.at[part], sems.at[len(copies)])
            )
    for copy in copies:
        copy.start()
    for copy in copies:
        copy.wait()


def begin_kernel(stream_ref, pend_ref, out_ref):
    out_ref[...] = (stream_ref[...].astype(F32) + pend_ref[...].astype(F32)).astype(BF16)


def choose_kernel(arrived_ref, moved_ref, out_ref):
    out_ref[...] = jnp.where(
        lax.axis_index("section") == 0, arrived_ref[...], moved_ref[...]
    )


def cut_kernel(count, wo_ref, *refs):
    blocks, sems = refs[:-1], refs[-1]
    half, shard = blocks[0].shape
    rows = pl.ds(pl.multiple_of(lax.axis_index("group") * half, half), half)
    copies = []
    for k in range(1, count):
        target = lax.rem(lax.axis_index("tensor") + k, count)
        columns = pl.ds(pl.multiple_of(target * shard, shard), shard)
        copies.append(
            pltpu.make_async_copy(wo_ref.at[rows, columns], blocks[k - 1], sems.at[k - 1])
        )
    for copy in copies:
        copy.start()
    for copy in copies:
        copy.wait()


def stack_kernel(*refs):
    out_ref = refs[-1]
    for k, block in enumerate(refs[:-1]):
        out_ref[k] = block[...]


def place_kernel(count, *refs):
    wo_ref = refs[0]
    got = refs[1:count]
    other_ref, weights, sems = refs[count:]
    me, half_index = lax.axis_index("tensor"), lax.axis_index("group")
    half, shard = got[0].shape
    begin = pl.multiple_of(half_index * half, half)
    rest = pl.multiple_of(half - half_index * half, half)
    columns = pl.ds(pl.multiple_of(me * shard, shard), shard)
    copies = [pltpu.make_async_copy(wo_ref.at[:, columns], weights.at[me], sems.at[0, 0])]
    for k in range(1, count):
        owner = owner_of(k, count)
        copies.append(
            pltpu.make_async_copy(
                got[k - 1], weights.at[owner, pl.ds(begin, half)], sems.at[0, k]
            )
        )
        copies.append(
            pltpu.make_async_copy(
                other_ref.at[k - 1], weights.at[owner, pl.ds(rest, half)], sems.at[1, k]
            )
        )
    for copy in copies:
        copy.start()
    for copy in copies:
        copy.wait()


def project_kernel(count, span, batch, *refs):
    parts = refs[: batch * count]
    gain_ref, wq_ref, wkv_ref, query_ref, same_ref, other_ref = refs[batch * count :]
    odd = lax.rem(lax.axis_index("tensor"), 2) == 1
    head = wq_ref.shape[1]
    rows, shard = parts[0].shape
    block = same_ref.shape[0] // batch
    for b in range(batch):
        own = parts[b * count : (b + 1) * count]
        total = jnp.zeros((rows, 1), F32)
        for part in own:
            values = part[...].astype(F32)
            total = total + jnp.sum(values * values, axis=-1, keepdims=True)
        scale = lax.rsqrt(total / (shard * count) + EPS)
        queries = jnp.zeros((rows, wq_ref.shape[1]), F32)
        keyval = jnp.zeros((rows, wkv_ref.shape[1]), F32)
        for k, part in enumerate(own):
            here = pl.ds(pl.multiple_of(owner_of(k, count) * shard, shard), shard)
            normed = (part[...].astype(F32) * scale * gain_ref[:, here]).astype(BF16)
            queries = queries + jnp.dot(normed, wq_ref[here, :], preferred_element_type=F32)
            keyval = keyval + jnp.dot(normed, wkv_ref[here, :], preferred_element_type=F32)
        queries = queries.astype(BF16)
        query_ref[b] = queries[:span]
        even_half, odd_half = keyval[:, :head], keyval[:, head:]
        for message_ref, is_odd in ((same_ref, odd), (other_ref, jnp.logical_not(odd))):
            message_ref[b * block : b * block + span] = jnp.where(
                is_odd, odd_half[:span], even_half[:span]
            ).astype(BF16)
            for n, rest in enumerate((even_half, odd_half, queries)):
                first = b * block + span + 8 * n
                message_ref[first : first + rows - span] = rest[span:].astype(BF16)


def attend_kernel(count, span, ticks, *refs):
    query_ref = refs[0]
    parts = refs[1 : 1 + count]
    segment_ref, length_ref, cache_ref, out_ref, blocks, small = refs[1 + count :]
    me = lax.axis_index("tensor")
    head = query_ref.shape[2]
    factor = 1.0 / math.sqrt(head)
    heads = count
    block = parts[0].shape[0] // len(ticks)
    for k, part in enumerate(parts):
        blocks[owner_of(k, count)] = part[...]
    small[...] = jnp.zeros_like(small)
    row_ids = lax.broadcasted_iota(jnp.int32, (span, span), 0)
    col_ids = lax.broadcasted_iota(jnp.int32, (span, span), 1)
    picked = lax.broadcasted_iota(jnp.int32, (count, head), 0) == me

    def own_row(rows):
        return jnp.sum(jnp.where(picked, rows.astype(F32), 0.0), axis=0, keepdims=True)

    for b, tick in enumerate(ticks):
        micro = tick - lax.axis_index("section") + lax.axis_size("section") - 1
        first = b * block
        out = b * (span + count)
        keys = blocks[lax.div(me, 2), first : first + span]
        values = blocks[heads // 2 + lax.div(me, 2), first : first + span]
        scores = (
            lax.dot_general(
                query_ref[b], keys, (((1,), (1,)), ((), ())), preferred_element_type=F32
            )
            * factor
        )
        across = segment_ref[pl.ds(micro, 1), :]
        down = jnp.sum(jnp.where(row_ids == col_ids, across, 0), axis=1, keepdims=True)
        scores = jnp.where((down == across) & (col_ids <= row_ids), scores, NEG)
        expo = jnp.exp(scores - jnp.max(scores, axis=-1, keepdims=True))
        weights = (expo / jnp.sum(expo, axis=-1, keepdims=True)).astype(BF16)
        out_ref[out : out + span] = jnp.dot(
            weights, values, preferred_element_type=F32
        ).astype(BF16)

        def new_row(device, n):
            start = first + span + 8 * n
            return own_row(blocks[device, start : start + count])

        for h in range(heads):
            small[b, 0, h : h + 1, :] = new_row(h, 2)
            small[b, 1, h : h + 1, :] = new_row(h // 2, h % 2)
            small[b, 2, h : h + 1, :] = new_row((heads + h) // 2, h % 2)
        queries = small[b, 0]
        line = lax.broadcasted_iota(jnp.int32, queries.shape, 0)
        spread = jnp.concatenate(
            [jnp.where(line == h, queries, 0.0) for h in range(heads)], axis=1
        ).astype(BF16)
        own = jnp.sum(queries * small[b, 1], axis=-1, keepdims=True) * factor
        dec_scores = (
            lax.dot_general(
                spread,
                cache_ref[tick, :, : heads * head],
                (((1,), (1,)), ((), ())),
                preferred_element_type=F32,
            )
            * factor
        )
        positions = lax.broadcasted_iota(jnp.int32, dec_scores.shape, 1)
        lanes = lax.broadcasted_iota(jnp.int32, length_ref.shape, 1)
        live = jnp.sum(jnp.where(lanes == micro, length_ref[...], 0), axis=1, keepdims=True)
        dec_scores = jnp.where(positions < live, dec_scores, NEG)
        top = jnp.maximum(jnp.max(dec_scores, axis=-1, keepdims=True), own)
        dec_expo = jnp.exp(dec_scores - top)
        own_expo = jnp.exp(own - top)
        total = jnp.sum(dec_expo, axis=-1, keepdims=True) + own_expo
        dec_weights = (dec_expo / total).astype(BF16)
        own_weight = (own_expo / total).astype(BF16).astype(F32)
        result = jnp.dot(dec_weights, cache_ref[tick, :, heads * head :], preferred_element_type=F32)
        extra = own_weight * small[b, 2]
        for h in range(heads):
            row = result[h : h + 1, h * head : (h + 1) * head] + extra[h : h + 1]
            small[b, 3, h : h + 1, :] = row
        out_ref[out + span : out + span + count] = small[b, 3, :heads].astype(BF16)


def summed_terms(count, span, first, parts, weights, scratch):
    rows_ref, decode, placed = scratch
    for k, part in enumerate(parts):
        owner = owner_of(k, count)
        rows_ref[owner, :span] = part[first : first + span]
        decode[owner, :count] = part[first + span : first + span + count].astype(F32)
    for h in range(count):
        for r in range(count):
            placed[h, r : r + 1, :] = decode[r, h : h + 1, :]
        rows_ref[h, span : span + count] = placed[h, :count].astype(BF16)
    def columns(part):
        total = None
        for h in range(count):
            term = jnp.dot(rows_ref[h], weights[h, :, part], preferred_element_type=F32)
            term = term.astype(BF16).astype(F32)
            total = term if total is None else total + term
        return total[: span + count].astype(BF16)

    return columns


def first_output_kernel(count, span, *refs):
    parts = refs[:count]
    weights, first_new, early, late, out_ref, one_ref, two_ref = refs[count : count + 7]
    section = lax.axis_index("section")
    sections = lax.axis_size("section")
    out_ref[...] = summed_terms(count, span, 0, parts, weights, refs[count + 7 :])(slice(None))
    fresh = (first_new[...].astype(F32) + out_ref[...].astype(F32)).astype(BF16)
    is_last = section == sections - 1
    one_ref[...] = jnp.where(is_last, early[...], fresh)
    two_ref[...] = jnp.where(
        section == sections - 2, late[...], jnp.where(is_last, early[...], fresh)
    )


def second_output_kernel(count, span, *refs):
    parts = refs[:count]
    weights, first_new, pend_first, second_new = refs[count : count + 4]
    out_ref, hist_stream, hist_pend = refs[count + 4 : count + 7]
    scratch = refs[count + 7 : -1]
    sems = refs[-1]
    copies = [
        pltpu.make_async_copy(first_new, hist_stream.at[0], sems.at[0]),
        pltpu.make_async_copy(second_new, hist_stream.at[1], sems.at[1]),
        pltpu.make_async_copy(pend_first, hist_pend.at[0], sems.at[2]),
    ]
    for copy in copies:
        copy.start()
    out_ref[...] = summed_terms(count, span, span + count, parts, weights, scratch)(slice(None))
    last = pltpu.make_async_copy(out_ref, hist_pend.at[1], sems.at[3])
    last.start()
    for copy in copies:
        copy.wait()
    last.wait()


def third_output_kernel(count, span, *refs):
    parts = refs[:count]
    weights, third, pend_in = refs[count : count + 3]
    hist_stream, hist_pend = refs[count + 5 : count + 7]
    scratch = refs[count + 7 : -3]
    fresh, result, sems = refs[-3:]
    fresh[...] = (third[...].astype(F32) + pend_in[...].astype(F32)).astype(BF16)
    copy = pltpu.make_async_copy(fresh, hist_stream.at[2], sems.at[0])
    copy.start()
    columns = summed_terms(count, span, 0, parts, weights, scratch)
    half = result.shape[1] // 2
    copies = [copy]
    for n in range(2):
        part = slice(n * half, (n + 1) * half)
        result[:, part] = columns(part)
        copies.append(
            pltpu.make_async_copy(result.at[:, part], hist_pend.at[2, :, part], sems.at[1 + n])
        )
        copies[-1].start()
    for copy in copies:
        copy.wait()


def fast_body(
    stream_in, pend_in, arrivals, norm_gain, wq, wkv, wo, cache, dec_len, span_seg
):
    count = lax.axis_size("tensor")
    rows, shard = stream_in.shape[1:]
    head = wq.shape[2]
    span = span_seg.shape[1]
    length = cache.shape[3]
    ticks = cache.shape[1]
    half = head // 2
    cached = cache.reshape(ticks, length, cache.shape[4])
    padded = (rows + 7) // 8 * 8
    message_rows = span + 24
    limit = pltpu.CompilerParams(vmem_limit_bytes=16 * 1024 * 1024)
    block = jax.ShapeDtypeStruct((rows, shard), BF16)
    history = jax.ShapeDtypeStruct((ticks, rows, shard), BF16)

    def cost(flops, moved_bytes):
        return pl.CostEstimate(
            flops=int(0 * flops), bytes_accessed=int(0 * moved_bytes), transcendentals=0
        )

    given = (norm_gain, wq[0], wkv[0], span_seg, dec_len.T, cached)
    pieces = (1, count, count, 1, 1, ticks)
    kept = pl.pallas_call(
        functools.partial(load_kernel, pieces),
        out_shape=tuple(jax.ShapeDtypeStruct(array.shape, array.dtype) for array in given),
        in_specs=[HBM] * len(given),
        out_specs=(VMEM,) * len(given),
        scratch_shapes=[pltpu.SemaphoreType.DMA((sum(pieces),))],
        compiler_params=limit,
        cost_estimate=cost(0, 4 * wq.shape[1] * 3 * head),
        name="load",
    )(*[in_hbm(array) for array in given])
    gain, wq_here, wkv_here, segments, lengths, cached = [in_vmem(array) for array in kept]

    def project(parts):
        batch = len(parts) // count
        return pl.pallas_call(
            functools.partial(project_kernel, count, span, batch),
            out_shape=(
                jax.ShapeDtypeStruct((batch, span, head), BF16),
                jax.ShapeDtypeStruct((batch * message_rows, head), BF16),
                jax.ShapeDtypeStruct((batch * message_rows, head), BF16),
            ),
            in_specs=[VMEM] * (batch * count + 3),
            out_specs=(VMEM, VMEM, VMEM),
            compiler_params=limit,
            cost_estimate=cost(
                2 * batch * rows * shard * count * 3 * head,
                2 * shard * count * (3 * head + rows),
            ),
            name="project",
        )(*[in_vmem(part) for part in parts], gain, wq_here, wkv_here)

    def attend(queries, parts, which):
        batch = len(which)
        return pl.pallas_call(
            functools.partial(attend_kernel, count, span, which),
            out_shape=jax.ShapeDtypeStruct((batch * (span + count), head), BF16),
            in_specs=[VMEM] * (count + 4),
            out_specs=VMEM,
            scratch_shapes=[
                pltpu.VMEM((count, batch * message_rows, head), BF16),
                pltpu.VMEM((batch, 4, 8, head), F32),
            ],
            compiler_params=limit,
            cost_estimate=cost(
                batch * 4 * 8 * length * 4 * head,
                batch * (4 * length * 4 * head + count * message_rows * 4 * head),
            ),
            name="attend",
        )(queries, *[in_vmem(part) for part in parts], segments, lengths, cached)

    def message_pieces(same, other):
        kinds = [same if k % 2 == 0 else other for k in range(count)]
        return [same] + [turned(kinds[k], "tensor", k) for k in range(1, count)]

    output_scratch = [
        pltpu.VMEM((count, padded, head), BF16),
        pltpu.VMEM((count, 8, head), F32),
        pltpu.VMEM((count, 8, head), F32),
    ]
    output_cost = cost(2 * rows * shard * count * head, 2 * shard * (count * head + rows))
    stream_parts = relayed_pieces_of(stream_in[0], "tensor")
    first_new = pl.pallas_call(
        begin_kernel,
        out_shape=block,
        in_specs=[VMEM] * 2,
        out_specs=VMEM,
        compiler_params=limit,
        cost_estimate=cost(0, 6 * rows * shard),
        name="begin",
    )(stream_in[0], pend_in[0])
    early, late = arrivals[0], arrivals[1]
    second = pl.pallas_call(
        choose_kernel,
        out_shape=block,
        in_specs=[VMEM] * 2,
        out_specs=VMEM,
        compiler_params=limit,
        cost_estimate=cost(0, 6 * rows * shard),
        name="choose",
    )(early, moved(first_new, "section", 1))
    second_parts = pieces_of(second, "tensor")
    queries, same, other_half = project(stream_parts + second_parts)
    message_parts = message_pieces(same, other_half)
    small_block = jax.ShapeDtypeStruct((half, shard), BF16)
    cut = pl.pallas_call(
        functools.partial(cut_kernel, count),
        out_shape=(small_block,) * (count - 1),
        in_specs=[HBM],
        out_specs=(VMEM,) * (count - 1),
        scratch_shapes=[pltpu.SemaphoreType.DMA((count - 1,))],
        compiler_params=limit,
        cost_estimate=cost(0, 4 * half * shard * count),
        name="cut",
    )(in_hbm(wo[0]))
    blocks = [
        turned(cut[0], "tensor", 1),
        turned(cut[1], "tensor", 2),
        turned(cut[2], "tensor", 3),
    ]
    stacked = pl.pallas_call(
        stack_kernel,
        out_shape=jax.ShapeDtypeStruct((count - 1, half, shard), BF16),
        in_specs=[VMEM] * (count - 1),
        out_specs=VMEM,
        compiler_params=limit,
        cost_estimate=cost(0, 4 * half * shard * count),
        name="stack",
    )(*[in_vmem(block_k) for block_k in blocks])
    given = (in_hbm(wo[0]), *blocks, turned(stacked, "group", 1))
    weights = in_vmem(
        pl.pallas_call(
            functools.partial(place_kernel, count),
            out_shape=jax.ShapeDtypeStruct((count, head, shard), BF16),
            in_specs=[ANY] * len(given),
            out_specs=VMEM,
            scratch_shapes=[pltpu.SemaphoreType.DMA((2, count))],
            compiler_params=limit,
            cost_estimate=cost(0, 4 * count * head * shard),
            name="place",
        )(*given)
    )
    attended = attend(queries, message_parts, (0, 1))
    attended_parts = pieces_of(attended, "tensor")
    pend_first, one_on, two_on = pl.pallas_call(
        functools.partial(first_output_kernel, count, span),
        out_shape=(block, block, block),
        in_specs=[VMEM] * (count + 4),
        out_specs=(VMEM, VMEM, VMEM),
        scratch_shapes=output_scratch,
        compiler_params=limit,
        cost_estimate=output_cost,
        name="output_first",
    )(
        *[in_vmem(part) for part in attended_parts],
        weights,
        in_vmem(first_new),
        in_vmem(early),
        in_vmem(late),
    )
    third = turned(two_on, "section", 2)
    third_parts = pieces_of(third, "tensor")
    second_new = turned(one_on, "section", 1)
    pend_second, hist_stream, hist_pend = pl.pallas_call(
        functools.partial(second_output_kernel, count, span),
        out_shape=(block, history, history),
        in_specs=[VMEM] * (count + 4),
        out_specs=(VMEM, HBM, HBM),
        scratch_shapes=output_scratch + [pltpu.SemaphoreType.DMA((4,))],
        compiler_params=limit,
        cost_estimate=output_cost,
        name="output_second",
    )(
        *[in_vmem(part) for part in attended_parts],
        weights,
        in_vmem(first_new),
        in_vmem(pend_first),
        in_vmem(second_new),
    )
    pend_last_in = moved(pend_second, "section", 1)
    queries, same, other_half = project(third_parts)
    message_parts = message_pieces(same, other_half)
    attended = attend(queries, message_parts, (2,))
    attended_parts = pieces_of(attended, "tensor")
    hist_stream, hist_pend = pl.pallas_call(
        functools.partial(third_output_kernel, count, span),
        out_shape=(history, history),
        in_specs=[VMEM] * (count + 3) + [HBM] * 2,
        out_specs=(HBM, HBM),
        scratch_shapes=output_scratch
        + [
            pltpu.VMEM((rows, shard), BF16),
            pltpu.VMEM((rows, shard), BF16),
            pltpu.SemaphoreType.DMA((3,)),
        ],
        input_output_aliases={count + 3: 0, count + 4: 1},
        compiler_params=limit,
        cost_estimate=output_cost,
        name="output_third",
    )(
        *[in_vmem(part) for part in attended_parts],
        weights,
        in_vmem(third),
        in_vmem(pend_last_in),
        hist_stream,
        hist_pend,
    )
    return hist_stream[None], hist_pend[None]


def passed_along(block, axis, distance):
    devices = range(lax.axis_size(axis))
    route = [(i - distance, i) for i in devices if i - distance in devices]
    return lax.ppermute(block, axis, route)


def rms_norm(stream, gain):
    values = stream.astype(jnp.float32)
    mean_sq = jnp.mean(values * values, axis=-1, keepdims=True)
    return (values * lax.rsqrt(mean_sq + EPS) * gain).astype(jnp.bfloat16)


def span_attention(queries, keys, values, segment):
    scale = 1.0 / math.sqrt(queries.shape[-1])
    scores = jnp.einsum("qd,kd->qk", queries, keys, preferred_element_type=jnp.float32) * scale
    count = segment.shape[0]
    rowsid = lax.broadcasted_iota(jnp.int32, (count, count), 0)
    colsid = lax.broadcasted_iota(jnp.int32, (count, count), 1)
    allowed = (segment[:, None] == segment[None, :]) & (colsid <= rowsid)
    scores = jnp.where(allowed, scores, NEG)
    top = jnp.max(scores, axis=-1, keepdims=True)
    expo = jnp.exp(scores - top)
    weights = (expo / jnp.sum(expo, axis=-1, keepdims=True)).astype(jnp.bfloat16)
    return jnp.dot(weights, values, preferred_element_type=jnp.float32).astype(jnp.bfloat16)


def decode_attention(queries, cache_keys, cache_values, new_keys, new_values, lengths):
    scale = 1.0 / math.sqrt(queries.shape[-1])
    scores = (
        jnp.einsum("rgjd,rcgd->rgjc", queries, cache_keys, preferred_element_type=jnp.float32)
        * scale
    )
    positions = lax.broadcasted_iota(jnp.int32, scores.shape, 3)
    scores = jnp.where(positions < lengths[:, None, None, None], scores, NEG)
    own = jnp.einsum("rgjd,rgd->rgj", queries, new_keys, preferred_element_type=jnp.float32) * scale
    top = jnp.maximum(jnp.max(scores, axis=-1), own)
    expo = jnp.exp(scores - top[..., None])
    own_expo = jnp.exp(own - top)
    total = jnp.sum(expo, axis=-1) + own_expo
    weights = (expo / total[..., None]).astype(jnp.bfloat16)
    own_weight = (own_expo / total).astype(jnp.bfloat16)
    result = jnp.einsum(
        "rgjc,rcgd->rgjd", weights, cache_values, preferred_element_type=jnp.float32
    )
    result = (
        result
        + own_weight.astype(jnp.float32)[..., None] * new_values.astype(jnp.float32)[:, :, None, :]
    )
    return result.astype(jnp.bfloat16)


def plain_body(stream_in, pend_in, arrivals, norm_gain, wq, wkv, wo, cache, dec_len, span_seg):
    tensor_count = lax.axis_size("tensor")
    section_count = lax.axis_size("section")
    tensor_index = lax.axis_index("tensor")
    section_index = lax.axis_index("section")
    row_count = stream_in.shape[1]
    shard = stream_in.shape[2]
    width = wq.shape[1]
    head_dim = wq.shape[2]
    kv_cols = cache.shape[4]
    kv_heads = kv_cols // (2 * head_dim)
    group_size = tensor_count // kv_heads
    span_rows = span_seg.shape[1]
    dec_rows = cache.shape[2]
    cache_len = cache.shape[3]
    tick_count = cache.shape[1]
    gain = norm_gain[0]
    kv_head = tensor_index // group_size
    stacked = jnp.concatenate([stream_in[0], pend_in[0], arrivals.reshape(-1, shard)], axis=0)
    gathered = lax.all_gather(stacked, "tensor", axis=1, tiled=True)
    stream = gathered[:row_count]
    pending = gathered[row_count : 2 * row_count]
    arrived = gathered[2 * row_count :].reshape(tick_count - 1, row_count, width)
    hist_stream = []
    hist_pend = []
    for tick in range(tick_count):
        micro = tick - section_index + section_count - 1
        lengths = lax.dynamic_index_in_dim(dec_len, micro, 0, keepdims=False)
        segment = lax.dynamic_index_in_dim(span_seg, micro, 0, keepdims=False)
        full_rows = stream
        normed = rms_norm(full_rows, gain)
        queries = jnp.dot(normed, wq[0], preferred_element_type=jnp.float32).astype(jnp.bfloat16)
        kv_part = jnp.dot(normed, wkv[0], preferred_element_type=jnp.float32).astype(jnp.bfloat16)
        keyval = lax.all_gather(kv_part, "tensor", axis=1, tiled=True)
        keys_all = keyval[:span_rows, : kv_heads * head_dim].reshape(span_rows, kv_heads, head_dim)
        values_all = keyval[:span_rows, kv_heads * head_dim :].reshape(
            span_rows, kv_heads, head_dim
        )
        own_keys = lax.dynamic_index_in_dim(keys_all, kv_head, 1, keepdims=False)
        own_values = lax.dynamic_index_in_dim(values_all, kv_head, 1, keepdims=False)
        span_out = span_attention(queries[:span_rows], own_keys, own_values, segment)
        dec_queries = queries[span_rows:].reshape(-1, 1, head_dim)
        row_queries = lax.all_to_all(dec_queries, "tensor", split_axis=0, concat_axis=1, tiled=True)
        row_queries = row_queries.reshape(dec_rows, kv_heads, group_size, head_dim)
        row_start = span_rows + tensor_index * dec_rows
        new_kv = lax.dynamic_slice_in_dim(keyval, row_start, dec_rows, 0)
        new_keys = new_kv[:, : kv_heads * head_dim].reshape(dec_rows, kv_heads, head_dim)
        new_values = new_kv[:, kv_heads * head_dim :].reshape(dec_rows, kv_heads, head_dim)
        cache_now = cache[0, tick]
        cache_keys = cache_now[:, :, : kv_heads * head_dim].reshape(
            dec_rows, cache_len, kv_heads, head_dim
        )
        cache_values = cache_now[:, :, kv_heads * head_dim :].reshape(
            dec_rows, cache_len, kv_heads, head_dim
        )
        row_out = decode_attention(
            row_queries, cache_keys, cache_values, new_keys, new_values, lengths
        )
        row_out = row_out.reshape(dec_rows, tensor_count, head_dim)
        dec_back = lax.all_to_all(
            row_out, "tensor", split_axis=1, concat_axis=0, tiled=True
        ).reshape(-1, head_dim)
        attended = jnp.concatenate([span_out, dec_back], axis=0)
        term = jnp.dot(attended, wo[0], preferred_element_type=jnp.float32).astype(jnp.bfloat16)
        pending_new = lax.psum(term, "tensor").astype(jnp.float32).astype(jnp.bfloat16)
        stream_new = (stream.astype(jnp.float32) + pending.astype(jnp.float32)).astype(jnp.bfloat16)
        hist_stream.append(lax.dynamic_slice_in_dim(stream_new, tensor_index * shard, shard, 1))
        hist_pend.append(lax.dynamic_slice_in_dim(pending_new, tensor_index * shard, shard, 1))
        if tick + 1 < tick_count:
            moved_stream, moved_pend = passed_along((stream_new, pending_new), "section", 1)
            first_section = section_index == 0
            stream = jnp.where(first_section, arrived[tick], moved_stream)
            pending = jnp.where(first_section, jnp.zeros_like(moved_pend), moved_pend)
    return (jnp.stack(hist_stream)[None], jnp.stack(hist_pend)[None])


def body(stream_in, pend_in, arrivals, norm_gain, wq, wkv, wo, cache, dec_len, span_seg):
    count = lax.axis_size("tensor")
    head = wq.shape[2]
    fits = (
        head == 128
        and lax.axis_size("group") == 2
        and cache.shape[1] == 3
        and cache.shape[2] == 1
        and cache.shape[4] == 2 * head * count
        and wkv.shape[2] == 2 * head
        and stream_in.shape[2] % 128 == 0
        and span_seg.shape[1] % 16 == 0
        and stream_in.shape[1] == span_seg.shape[1] + count
        and count == 4
    )
    chosen = fast_body if fits else plain_body
    return chosen(
        stream_in, pend_in, arrivals, norm_gain, wq, wkv, wo, cache, dec_len, span_seg
    )


def solution(mesh):
    return jax.shard_map(
        body,
        mesh=mesh,
        in_specs=(
            P("section", "group", "tensor"),
            P("section", "group", "tensor"),
            P(None, "group", "tensor"),
            P("section", None),
            P("section", None, "tensor"),
            P("section", None, "tensor"),
            P("section", "tensor", None),
            P("section", "group", "tensor", None, None),
            P("group", "tensor"),
            P("group", None),
        ),
        out_specs=(P("section", None, "group", "tensor"), P("section", None, "group", "tensor")),
        check_vma=False,
    )
```
